32 devices in a mesh: proj: 4 (over x, core), scen: 8 (over z, y).
Axes of the slice: x: 2, y: 2, z: 4, core: 2. Of those that a mesh axis runs over, the one named last changes fastest.
Arguments:
- fund_value: float32 [4096, 1024], P('proj', 'scen'), may hold values from 0.5 to 2
- in_force: float32 [4096, 1024], P('proj', 'scen'), may hold values from 0.5 to 1.5
- guarantee_base: float32 [4096, 1024], P('proj', 'scen'), may hold values from 0.5 to 2
- lapse_rate: float32 [4096, 1024], P('proj', 'scen'), may hold values from 0.02 to 0.4
- cohort: int32 [4096], P('proj'), may hold values from 0 to 511, as said below
- product: int32 [4096], P('proj'), may hold values from 0 to 15
- guarantee_type: int32 [4096], P('proj'), may hold values from 0 to 3
- returns: float32 [8, 12, 1024], P(None, None, 'scen'), may hold values from -0.625 to 0.625
- mix_table: float32 [16, 8], replicated, may hold values from 0.05 to 1
- fee_table: float32 [4], replicated, may hold values from 0.001 to 0.01
- rollup_table: float32 [4], replicated, may hold values from 0.01 to 0.08
- fund_vol: float32 [8], replicated, may hold values from 0.15 to 0.6
- closing_sigma_figure: float32 [1024], P('scen'), may hold values from 0.5 to 2
- shocks: float32 [8, 2, 1024], P(None, None, 'scen'), may hold values from -6 to 6
- base_table: float32 [10, 16], replicated, may hold values from 0.03 to 0.2
- year_index: int32 [1], replicated, may hold values from 0 to 9
Outputs:
- fund_next: float32 [4096, 1024], P('proj', 'scen')
- force_next: float32 [4096, 1024], P('proj', 'scen')
- base_next: float32 [4096, 1024], P('proj', 'scen')
- lapse_next: float32 [4096, 1024], P('proj', 'scen')
- benefit_cost_per_account: float32 [512, 1024], P('proj', 'scen')
The draws below stay inside these ranges and needn't reach their ends.
Inputs may be any that keep to these rules, and one draw needn't show every extreme that they name: Each cohort holds exactly 8 model points; the model points of each index of proj include exactly 256 whose cohorts lie in the block of 128 cohorts that any one index of proj owns (cohorts q * 128 onward for index q).
All inputs are finite; a program needn't handle non-finite values.
Results may differ from the reference program's by a relative error of at most 0.00026.
Values sent between devices are 32-bit elements; how exact they have to be, the bound alone decides.
No kernel may reach another device: no remote copies, remote signals or barrier semaphores. Data moves between devices by JAX's collectives and lax.ppermute only.
A program may use at most 64 MiB of HBM per device.

```python
import math
import jax
import jax.numpy as jnp
from jax import lax

MP_DEV = 1024
COHORTS = 512
FUNDS = 8
VALUATION_TRIALS = 1024
HORIZON = 2
MONTHS = 12
PRODUCTS = 16
GTYPES = 4
YEARS = 10
MODEL_POINTS = 4096
SCENARIOS = 1024
N_PROJ = 4


def draw_cohort(key, part):
    block = COHORTS // N_PROJ
    share = MP_DEV // N_PROJ
    labels = (jnp.arange(MP_DEV, dtype=jnp.int32) % block).astype(jnp.int32)
    owners = jnp.arange(N_PROJ, dtype=jnp.int32)

    def owner_labels(owner):
        return jax.random.permutation(jax.random.fold_in(key, owner), labels)
    spread_labels = jax.vmap(owner_labels)(owners)
    spread_labels = spread_labels + (owners * block)[:, None]
    placed = spread_labels.reshape(N_PROJ, N_PROJ, share).transpose(1, 0, 2).reshape(N_PROJ, MP_DEV)

    def device_order(device, row):
        return jax.random.permutation(jax.random.fold_in(key, device + 7919), row)
    mixed = jax.vmap(device_order)(owners, placed)
    return mixed.reshape(MODEL_POINTS).astype(jnp.int32)


def with_ends(result, stream_key, low, high):
    dims = result.shape
    spot = [jax.random.randint(jax.random.fold_in(stream_key, axis), (), 0, dims[axis]) for axis in range(len(dims))]
    result = result.at[tuple(spot)].set(low)
    longest = dims.index(max(dims))
    spot[longest] = (spot[longest] + 1) % dims[longest]
    return result.at[tuple(spot)].set(high)


def shard_levels(own_key, shape, cuts, low, high):
    level, own = 1.0, jax.random.fold_in(own_key, 6)
    for axis_at, parts in cuts:
        steps = jnp.exp(jax.random.uniform(jax.random.fold_in(own, axis_at), (parts,), jnp.float32, low / len(cuts), high / len(cuts)))
        level = level * jnp.repeat(steps, shape[axis_at] // parts).reshape([-1 if axis == axis_at else 1 for axis in range(len(shape))])
    return level


def normal_values(key, shape, spread, most, cuts=(), kind=jnp.bfloat16):
    level = shard_levels(key, shape, cuts, -0.22, 0.18) if cuts else 1.0
    values = jax.random.normal(key, shape, jnp.float32) * spread * level
    return jnp.minimum(jnp.maximum(values, -most), most).astype(kind)


def setup_inputs(seed: int = 0) -> dict:
    keys = jax.random.split(jax.random.key(seed), 17)
    fund_value = jnp.clip(jnp.exp(math.log(2.0) - 1.3862944 * jax.random.uniform(keys[0], (MODEL_POINTS, SCENARIOS), jnp.float32) ** shard_levels(keys[0], (MODEL_POINTS, SCENARIOS), ((0, 4), (1, 8)), -0.2, 0.2)), 0.5, 2.0)
    in_force = jnp.clip(0.5 + 1.0 * jax.random.uniform(keys[1], (MODEL_POINTS, SCENARIOS), jnp.float32) ** shard_levels(keys[1], (MODEL_POINTS, SCENARIOS), ((0, 4), (1, 8)), -0.2, 0.2), 0.5, 1.5)
    guarantee_base = jnp.clip(jnp.exp(math.log(2.0) - 1.3862944 * jax.random.uniform(keys[2], (MODEL_POINTS, SCENARIOS), jnp.float32) ** shard_levels(keys[2], (MODEL_POINTS, SCENARIOS), ((0, 4), (1, 8)), -0.2, 0.2)), 0.5, 2.0)
    lapse_rate = jnp.clip(0.02 + 0.38 * jax.random.uniform(keys[3], (MODEL_POINTS, SCENARIOS), jnp.float32) ** shard_levels(keys[3], (MODEL_POINTS, SCENARIOS), ((0, 4), (1, 8)), -0.2, 0.2), 0.02, 0.4)
    cohort = draw_cohort(jax.random.fold_in(keys[16], 71), 0)
    product = with_ends(jax.random.randint(keys[5], (MODEL_POINTS,), 0, PRODUCTS), jax.random.fold_in(keys[5], 1), 0, PRODUCTS - 1).astype(jnp.int32)
    guarantee_type = with_ends(jax.random.randint(keys[6], (MODEL_POINTS,), 0, GTYPES), jax.random.fold_in(keys[6], 1), 0, GTYPES - 1).astype(jnp.int32)
    returns = normal_values(keys[7], (FUNDS, MONTHS, SCENARIOS), 0.04, 0.625, ((2, 8),), jnp.float32)
    mix_table = jnp.clip(jnp.exp(jax.random.uniform(keys[8], (PRODUCTS, FUNDS), jnp.float32, math.log(0.05), math.log(1.0))), 0.05, 1.0)
    fee_table = jnp.clip(jnp.exp(jax.random.uniform(keys[9], (GTYPES,), jnp.float32, math.log(0.001), math.log(0.01))), 0.001, 0.01)
    rollup_table = jnp.clip(jnp.exp(jax.random.uniform(keys[10], (GTYPES,), jnp.float32, math.log(0.01), math.log(0.08))), 0.01, 0.08)
    fund_vol = jnp.clip(jnp.exp(jax.random.uniform(keys[11], (FUNDS,), jnp.float32, math.log(0.15), math.log(0.6))), 0.15, 0.6)
    closing_sigma_figure = jnp.clip(jnp.exp(math.log(2.0) - 1.3862944 * jax.random.uniform(keys[12], (SCENARIOS,), jnp.float32) ** shard_levels(keys[12], (SCENARIOS,), ((0, 8),), -0.2, 0.2)), 0.5, 2.0)
    shocks = normal_values(keys[13], (FUNDS, HORIZON, VALUATION_TRIALS), 1.0, 6.0, ((2, 8),), jnp.float32)
    base_table = jnp.clip(jnp.exp(jax.random.uniform(keys[14], (YEARS, PRODUCTS), jnp.float32, math.log(0.03), math.log(0.2))), 0.03, 0.2)
    year_index = jax.random.randint(keys[15], (1,), 0, YEARS).astype(jnp.int32)
    return dict(fund_value=fund_value, in_force=in_force, guarantee_base=guarantee_base, lapse_rate=lapse_rate, cohort=cohort, product=product, guarantee_type=guarantee_type, returns=returns, mix_table=mix_table, fee_table=fee_table, rollup_table=rollup_table, fund_vol=fund_vol, closing_sigma_figure=closing_sigma_figure, shocks=shocks, base_table=base_table, year_index=year_index)


HIGHEST = lax.Precision.HIGHEST
discount_rate = 0.96
lapse_floor = 0.3
lapse_span = 2.0
lapse_slope = 5.0
lapse_pivot = 0.4


def project(fund_value, in_force, guarantee_base, lapse_rate, mix_rows, fee_rows, rollup_rows, returns):
    keep_fee = (1.0 - fee_rows)[:, None]
    rollup_month = (1.0 + rollup_rows / 12.0)[:, None]
    survive = 1.0 - lapse_rate / 12.0
    for month_step in range(returns.shape[1]):
        growth = 1.0 + jnp.dot(mix_rows, returns[:, month_step, :], precision=HIGHEST, preferred_element_type=jnp.float32)
        fund_value = fund_value * growth * keep_fee
        guarantee_base = jnp.maximum(guarantee_base * rollup_month, fund_value)
        in_force = in_force * survive
    return fund_value, in_force, guarantee_base


def price_rows(scenario_conditions, sigma_figures, embedded_trials):
    factor_count, horizon_count, path_count = embedded_trials.shape
    span_cols = horizon_count * path_count
    flat_paths = embedded_trials.reshape(factor_count, span_cols)
    horizon = jnp.repeat(jnp.arange(1, horizon_count + 1, dtype=jnp.float32), path_count)
    weights = discount_rate ** horizon
    entry_number_overall = scenario_conditions.shape[1]
    target = max(1, (1 << 20) // span_cols)
    block_rows = math.gcd(entry_number_overall, 1 << (target.bit_length() - 1))
    block_count = entry_number_overall // block_rows
    benefit_strike_share = scenario_conditions[0].reshape(block_count, block_rows)
    fund_loads = scenario_conditions[1:]
    distributed_amounts = jnp.sum(fund_loads * fund_loads, axis=0).reshape(block_count, block_rows)
    cohort_sorted_entries = fund_loads.reshape(factor_count, block_count, block_rows).transpose(1, 0, 2)
    sigma_entries = sigma_figures.reshape(block_count, block_rows)

    def valuation_batch(fragment_list):
        money_rows, load_rows, level_part, spread_rows = fragment_list
        shifted = lax.dot_general(flat_paths, load_rows, (((0,), (0,)), ((), ())), precision=HIGHEST, preferred_element_type=jnp.float32)
        exponent = level_part[None, :] * shifted - 0.5 * (level_part * level_part)[None, :] * horizon[:, None] * spread_rows[None, :]
        payoff = jnp.maximum(money_rows[None, :] - jnp.exp(exponent), 0.0)
        return jnp.dot(weights, payoff, precision=HIGHEST)

    valued_amounts = lax.map(valuation_batch, (benefit_strike_share, cohort_sorted_entries, sigma_entries, distributed_amounts))
    return valued_amounts.reshape(entry_number_overall)


def valuation_conditions(scenario_conditions, sigma_figures, embedded_trials):
    cohort_count, columns, scen_count = scenario_conditions.shape
    flat_states = scenario_conditions.transpose(1, 2, 0).reshape(columns, scen_count * cohort_count)
    sigma_entries = jnp.repeat(sigma_figures, cohort_count)
    return price_rows(flat_states, sigma_entries, embedded_trials).reshape(scen_count, cohort_count)


def reference(fund_value, in_force, guarantee_base, lapse_rate, cohort, product, guarantee_type, returns, mix_table, fee_table, rollup_table, fund_vol, closing_sigma_figure, shocks, base_table, year_index):
    mix_norm = mix_table / jnp.sum(mix_table, axis=1, keepdims=True)
    mix_rows = mix_norm[product]
    fee_rows = fee_table[guarantee_type]
    rollup_rows = rollup_table[guarantee_type]
    fund_next, force_next, base_next = project(fund_value, in_force, guarantee_base, lapse_rate, mix_rows, fee_rows, rollup_rows, returns)
    weighted = force_next * fund_next
    value_sum = jax.ops.segment_sum(weighted, cohort, num_segments=COHORTS)
    guarantee_sum = jax.ops.segment_sum(force_next * base_next, cohort, num_segments=COHORTS)
    mix_sums = jnp.stack([jax.ops.segment_sum(weighted * mix_rows[:, factor][:, None], cohort, num_segments=COHORTS) for factor in range(FUNDS)], axis=1)
    scenario_conditions = jnp.concatenate([(guarantee_sum / value_sum)[:, None, :], mix_sums / value_sum[:, None, :] * fund_vol[None, :, None]], axis=1)
    embedded_trials = jnp.cumsum(shocks, axis=1)
    valued_amounts = valuation_conditions(scenario_conditions, closing_sigma_figure, embedded_trials)
    benefit_cost_per_account = valued_amounts.T / VALUATION_TRIALS
    cost_rows = benefit_cost_per_account[cohort]
    base_lapse = base_table[year_index[0]][product]
    lapse_next = base_lapse[:, None] * (lapse_floor + lapse_span * jax.nn.sigmoid(lapse_slope * (lapse_pivot - cost_rows)))
    return fund_next, force_next, base_next, lapse_next, benefit_cost_per_account
```

```python
import functools
import math

import jax
import jax.numpy as jnp
from jax import lax
from jax.experimental import pallas as pl
from jax.experimental.pallas import tpu as pltpu
from jax.sharding import PartitionSpec as P

COHORTS = 512
MONTHS_PER_YEAR = 12.0
DISCOUNT = 0.96
LAPSE_FLOOR, LAPSE_SPAN, LAPSE_SLOPE, LAPSE_PIVOT = 0.3, 2.0, 5.0, 0.4
LOG2E = 1.0 / math.log(2.0)
LANES = 128
DEPTH = 64
HIGHEST = lax.Precision.HIGHEST
F32, BF16, I32 = jnp.float32, jnp.bfloat16, jnp.int32
VMEM = pl.BlockSpec(memory_space=pltpu.VMEM)
SMEM = pl.BlockSpec(memory_space=pltpu.SMEM)
HBM = pl.BlockSpec(memory_space=pl.ANY)


def dot(a, b):
    return jnp.dot(a, b, preferred_element_type=F32)


def iota(shape, axis):
    return lax.broadcasted_iota(I32, shape, axis)


def split(x, parts):
    out = []
    for _ in range(parts):
        top = x.astype(BF16).astype(F32)
        out.append(top)
        x = x - top
    return out


def halves(x):
    return jnp.concatenate(split(x, 2), axis=1).astype(BF16)


def join(x):
    return x[:, :LANES] + x[:, LANES:]


def relabel(cohort, owned, me):
    shift = owned.bit_length() - 1
    owner = jnp.bitwise_xor(lax.shift_right_logical(cohort, shift), me)
    return owner, lax.shift_left(owner, shift) + jnp.bitwise_and(cohort, owned - 1)


def project_kernel(dims, me_ref, year_ref, fee_ref, roll_ref, cohort_ref, product_ref, type_ref, mix_ref, base_ref,
                   returns_ref, fund_hbm, force_hbm, guar_hbm, lapse_hbm, *rest):
    n_proj, owned, rows, months, products, types, chunk = dims
    sends = rest[:n_proj]
    (level_ref, fund_out, force_out, guar_out, fund, force, guar, lapse, table, hot, weighted, secured,
     in_sem, out_sem) = rest[n_proj:]
    points = fund.shape[0]
    blocks = points // LANES
    combos = products * types
    sources = ((fund_hbm, fund), (force_hbm, force), (guar_hbm, guar), (lapse_hbm, lapse))
    sinks = ((fund, fund_out), (force, force_out), (guar, guar_out))

    def fetch(i, a):
        span = pl.ds(i * chunk, chunk)
        return pltpu.make_async_copy(sources[a][0].at[span], sources[a][1].at[span], in_sem.at[i, a])

    def flush(i, a):
        span = pl.ds(i * chunk, chunk)
        return pltpu.make_async_copy(sinks[a][0].at[span], sinks[a][1].at[span], out_sem.at[i, a])

    chunks = points // chunk
    for i in range(chunks):
        for a in range(4):
            fetch(i, a).start()

    combo_product = lax.shift_right_logical(iota((combos, products), 0), types.bit_length() - 1)
    pick = (combo_product == iota((combos, products), 1)).astype(F32)
    mix = mix_ref[...]
    mix = mix / jnp.sum(mix, axis=1, keepdims=True)
    mix = jnp.dot(pick, mix, precision=HIGHEST, preferred_element_type=F32)
    combo_type = jnp.bitwise_and(iota((combos, LANES), 0), types - 1)
    fee = jnp.zeros((combos, LANES), F32)
    roll = jnp.zeros((combos, LANES), F32)
    for g in range(types):
        fee = jnp.where(combo_type == g, fee_ref[g], fee)
        roll = jnp.where(combo_type == g, roll_ref[g], roll)
    keep = 1.0 - fee

    def put(column, value):
        for i, part in enumerate(split(value, 3)):
            table[i * combos:(i + 1) * combos, column * LANES:(column + 1) * LANES] = part.astype(BF16)

    for t in range(months):
        growth = 1.0 + jnp.dot(mix, returns_ref[t], precision=HIGHEST, preferred_element_type=F32)
        put(t, growth * keep)
    put(months, 1.0 + roll / MONTHS_PER_YEAR)
    level = jnp.sum(pick * base_ref[pl.ds(year_ref[0], 1), :], axis=1, keepdims=True)
    put(months + 1, jnp.broadcast_to(level, (combos, LANES)))

    combo = (product_ref[...] * types + type_ref[...]).astype(F32).T
    slot = jnp.bitwise_and(iota((LANES, 3 * combos), 1), combos - 1).astype(F32)
    for b in range(blocks):
        column = jnp.broadcast_to(combo[:, b:b + 1], (LANES, 3 * combos))
        hot[b * LANES:(b + 1) * LANES, :] = (column == slot).astype(BF16)

    owner, label = relabel(cohort_ref[...], owned, me_ref[0])
    masks = jnp.concatenate([(owner == q).astype(F32) for q in range(n_proj)], axis=0)
    lower = (iota((LANES, LANES), 0) < iota((LANES, LANES), 1)).astype(BF16)
    before = dot(masks.astype(BF16), lower)
    count = dot(masks.astype(BF16), jnp.ones((LANES, LANES), BF16))
    size = n_proj * blocks
    r, c = iota((size, size), 0), iota((size, size), 1)
    shift = blocks.bit_length() - 1
    ahead = (lax.shift_right_logical(r, shift) == lax.shift_right_logical(c, shift)) & (c < r)
    before = before + dot(ahead.astype(BF16), count.astype(BF16))
    place = jnp.zeros((blocks, LANES), F32)
    for q in range(n_proj):
        span = slice(q * blocks, (q + 1) * blocks)
        place = place + masks[span] * (before[span] + float(q * rows))
    place = place.astype(I32)

    for i in range(chunks):
        for a in range(4):
            fetch(i, a).wait()
        for b in range(i * chunk // LANES, (i + 1) * chunk // LANES):
            span = slice(b * LANES, (b + 1) * LANES)
            factors = dot(hot[span, :], table[...])
            f, g = fund[span, :], guar[span, :]
            grow = factors[:, months * LANES:(months + 1) * LANES]
            level_ref[span, :] = factors[:, (months + 1) * LANES:]
            for t in range(months):
                f = f * factors[:, t * LANES:(t + 1) * LANES]
                g = jnp.maximum(g * grow, f)
            stay = 1.0 - lapse[span, :] / MONTHS_PER_YEAR
            stay = stay * stay * stay
            stay = stay * stay
            n = force[span, :] * (stay * stay)
            fund[span, :] = f
            guar[span, :] = g
            force[span, :] = n
            weighted[span, :] = halves(n * f)
            secured[span, :] = halves(n * g)
        for a in range(3):
            flush(i, a).start()

    facts = [jnp.zeros((16, LANES), F32)] * blocks
    local = jnp.bitwise_and(cohort_ref[...], owned - 1).astype(F32)
    kind = product_ref[...].astype(F32)
    which = iota((16, LANES), 0)
    facts = jnp.concatenate(
        [jnp.where(which == 0, kind[b:b + 1], jnp.where(which == 1, local[b:b + 1], 0.0)) for b in range(blocks)],
        axis=1).astype(BF16)
    for o in list(range(1, n_proj))[::-1] + [0]:
        send = sends[o]
        move = jnp.concatenate(
            [(iota((rows, LANES), 0) + o * rows == place[b:b + 1]).astype(BF16) for b in range(blocks)], axis=1)
        send[:rows, :] = join(dot(move, weighted[...]))
        group = jnp.concatenate(
            [(iota((owned, LANES), 0) + o * owned == label[b:b + 1]).astype(BF16) for b in range(blocks)], axis=1)
        send[rows:rows + owned, :] = join(dot(group, secured[...]))
        told = lax.dot_general(facts, move, (((1,), (1,)), ((), ())), preferred_element_type=F32)
        for b in range(rows // LANES):
            start = rows + owned + 8 * b
            send[start:start + 8, :] = told[:8, b * LANES:(b + 1) * LANES]

    for i in range(chunks):
        for a in range(3):
            flush(i, a).wait()


def hot_kernel(owned, me_ref, cohort_ref, hot_ref):
    _, label = relabel(cohort_ref[...], owned, me_ref[0])
    label = label.astype(F32).T
    slot = iota((LANES, hot_ref.shape[1]), 1).astype(F32)
    for b in range(hot_ref.shape[0] // LANES):
        column = jnp.broadcast_to(label[:, b:b + 1], slot.shape)
        hot_ref[b * LANES:(b + 1) * LANES, :] = (column == slot).astype(BF16)


def paths_kernel(horizon, shocks_ref, paths_ref):
    funds = shocks_ref.shape[0] // horizon
    count = shocks_ref.shape[1]
    which = iota((2 * funds, LANES), 0)
    for b in range(count // LANES):
        total = jnp.zeros((funds, LANES), F32)
        for h in range(horizon):
            total = total + shocks_ref[h * funds:(h + 1) * funds, b * LANES:(b + 1) * LANES]
            p1, p2, p3 = split(total, 3)
            ones = jnp.where(which < 3, float(h + 1), jnp.where(which < 6, 1.0, 0.0))
            full = jnp.concatenate([p1, p1, p2, p2, p3, p1, ones], axis=0)
            start = h * count + b * LANES
            paths_ref[start:start + LANES, :] = full.T.astype(BF16)


def value_kernel(dims, vol_ref, sigma_ref, mix_ref, paths_ref, *rest):
    n_proj, owned, rows, horizon, group, step = dims
    received = rest[:n_proj]
    cost_ref, weighted, mixes, loads, money = rest[n_proj:]
    products, funds = mix_ref.shape
    trials = paths_ref.shape[0] // horizon
    per = rows // LANES
    mix = mix_ref[...]
    mix = mix / jnp.sum(mix, axis=1, keepdims=True)
    tops, lows = [], []
    labels = []
    for o in range(n_proj):
        weighted[o * rows:(o + 1) * rows, :] = halves(received[o][:rows, :])
        for b in range(per):
            start = rows + owned + 8 * b
            facts = received[o][start:start + 8, :]
            hot = (jnp.broadcast_to(facts[0:1], (products, LANES)).astype(I32) == iota((products, LANES), 0)).astype(F32)
            share = lax.dot_general(mix, hot, (((0,), (0,)), ((), ())), precision=HIGHEST, preferred_element_type=F32)
            top, low = split(share, 2)
            tops.append(top)
            lows.append(low)
            labels.append(facts[1:2].astype(I32))
    spans = n_proj * per
    for b in range(spans):
        mixes[0, b] = tops[b]
        mixes[1, b] = lows[b]
    vol = jnp.zeros((funds, LANES), F32)
    for f in range(funds):
        vol = jnp.where(iota((funds, LANES), 0) == f, vol_ref[f], vol)
    sigma = sigma_ref[...]
    scale = sigma * LOG2E
    slope = -0.5 * sigma * sigma * LOG2E
    which = iota((funds, LANES), 0)

    def prepare(i, _):
        first = i * group
        sides = []
        for part in range(2):
            wide = []
            for b in range(spans):
                share = mixes[part, b]
                wide.append(jnp.concatenate(
                    [jnp.where(labels[b] == first + c, share, 0.0) for c in range(group)], axis=0).astype(BF16))
            sides.append(jnp.concatenate(wide, axis=1))
        sums = join(dot(sides[0], weighted[...]) + dot(sides[1], weighted[...]))
        span = pl.ds(pl.multiple_of(rows + first, 8), group)
        secured = received[0][span, :]
        for o in range(1, n_proj):
            secured = secured + received[o][span, :]
        for c in range(group):
            part = sums[c * funds:(c + 1) * funds]
            inverse = 1.0 / jnp.sum(part, axis=0, keepdims=True)
            load = part * inverse * vol
            ratio = secured[c:c + 1] * inverse
            money[pl.ds(first + c, 1), :] = ratio
            spread = jnp.sum(load * load, axis=0, keepdims=True)
            w1, w2, w3 = split(load * scale, 3)
            d = split(slope * spread, 3) + split(-LOG2E * jnp.log(ratio), 3)
            extra = jnp.zeros((funds, LANES), F32)
            for k in range(6):
                extra = jnp.where(which == k, d[k], extra)
            full = jnp.concatenate([w1, w2, w1, w2, w1, w3, extra, jnp.zeros_like(extra)], axis=0)
            loads[i, :, c * LANES:(c + 1) * LANES] = full.astype(BF16)
        return 0

    lax.fori_loop(0, owned // group, prepare, 0)

    def value(i, _):
        right = loads[i]
        total = None
        for h in range(horizon):
            reach = jnp.zeros((8, group * LANES), F32)
            for s in range(trials // step):
                left = paths_ref[h * trials + s * step:h * trials + (s + 1) * step, :]
                kept = jnp.exp2(jnp.minimum(dot(left, right), 0.0))
                reach = reach + jnp.sum(kept.reshape(step // 8, 8, group * LANES), axis=0)
            part = (float(trials) - jnp.sum(reach, axis=0, keepdims=True)) * (DISCOUNT ** (h + 1) / trials)
            total = part if total is None else total + part
        for c in range(group):
            row = pl.ds(i * group + c, 1)
            cost_ref[row, :] = total[:, c * LANES:(c + 1) * LANES] * money[row, :]
        return 0

    lax.fori_loop(0, owned // group, value, 0)


def lapse_kernel(n_proj, hot_ref, level_ref, *rest):
    costs, out_ref = rest[:n_proj], rest[n_proj]
    factors = jnp.concatenate(
        [halves(LAPSE_FLOOR + LAPSE_SPAN * jax.nn.sigmoid(LAPSE_SLOPE * (LAPSE_PIVOT - cost[...]))) for cost in costs],
        axis=0)
    for b in range(out_ref.shape[0] // LANES):
        span = slice(b * LANES, (b + 1) * LANES)
        out_ref[span, :] = level_ref[span, :] * join(dot(hot_ref[span, :], factors))


def flips(n, offset):
    return [(i, i ^ offset) for i in range(n)]


def body(fund_value, in_force, guarantee_base, lapse_rate, cohort, product, guarantee_type, returns, mix_table,
         fee_table, rollup_table, fund_vol, closing_sigma_figure, shocks, base_table, year_index):
    n_proj, n_scen = lax.axis_size("proj"), lax.axis_size("scen")
    points, width = fund_value.shape
    funds, months, _ = returns.shape
    horizon = shocks.shape[1]
    products, types = mix_table.shape[0], fee_table.shape[0]
    owned = COHORTS // n_proj
    rows = -(-points // n_proj // LANES) * LANES
    message = rows + owned + 8 * (rows // LANES)
    blocks = points // LANES
    me = lax.axis_index("proj").astype(I32).reshape(1)
    plane = jax.ShapeDtypeStruct((points, width), F32)
    chunk = 2 * LANES
    labels = cohort.reshape(blocks, LANES)

    outs = pl.pallas_call(
        functools.partial(project_kernel, (n_proj, owned, rows, months, products, types, chunk)),
        out_shape=[jax.ShapeDtypeStruct((message, width), F32)] * n_proj + [plane] * 4,
        in_specs=[SMEM] * 4 + [VMEM] * 6 + [HBM] * 4,
        out_specs=[VMEM] * n_proj + [VMEM] + [HBM] * 3,
        scratch_shapes=[pltpu.VMEM((points, width), F32)] * 4 + [
            pltpu.VMEM((3 * products * types, (months + 2) * LANES), BF16),
            pltpu.VMEM((points, 3 * products * types), BF16),
            pltpu.VMEM((points, 2 * width), BF16),
            pltpu.VMEM((points, 2 * width), BF16),
            pltpu.SemaphoreType.DMA((points // chunk, 4)),
            pltpu.SemaphoreType.DMA((points // chunk, 3)),
        ],
        name="project",
    )(me, year_index, fee_table, rollup_table, labels, product.reshape(blocks, LANES),
      guarantee_type.reshape(blocks, LANES), mix_table, base_table, returns.transpose(1, 0, 2),
      fund_value, in_force, guarantee_base, lapse_rate)
    sends, (level, fund_next, force_next, base_next) = outs[:n_proj], outs[n_proj:]

    received = [sends[0]] + [lax.ppermute(sends[o], "proj", flips(n_proj, o)) for o in range(1, n_proj)]

    paths = shocks.transpose(1, 0, 2).reshape(horizon * funds, shocks.shape[2])
    offset = 1
    while offset < n_scen:
        paths = jnp.concatenate([paths, lax.ppermute(paths, "scen", flips(n_scen, offset))], axis=1)
        offset *= 2
    trials = paths.shape[1]

    hot = pl.pallas_call(
        functools.partial(hot_kernel, owned),
        out_shape=jax.ShapeDtypeStruct((points, COHORTS), BF16),
        in_specs=[SMEM, VMEM], out_specs=VMEM, name="cohort_hot",
    )(me, labels)
    left = pl.pallas_call(
        functools.partial(paths_kernel, horizon),
        out_shape=jax.ShapeDtypeStruct((horizon * trials, DEPTH), BF16),
        in_specs=[VMEM], out_specs=VMEM, name="paths",
    )(paths)

    group = 16
    cost = pl.pallas_call(
        functools.partial(value_kernel, (n_proj, owned, rows, horizon, group, 64)),
        out_shape=jax.ShapeDtypeStruct((owned, width), F32),
        in_specs=[SMEM] + [VMEM] * (3 + n_proj), out_specs=VMEM,
        scratch_shapes=[
            pltpu.VMEM((n_proj * rows, 2 * width), BF16),
            pltpu.VMEM((2, n_proj * rows // LANES, funds, LANES), F32),
            pltpu.VMEM((owned // group, DEPTH, group * LANES), BF16),
            pltpu.VMEM((owned, width), F32),
        ],
        name="value",
    )(fund_vol, closing_sigma_figure.reshape(1, width), mix_table, left, *received)

    costs = [cost] + [lax.ppermute(cost, "proj", flips(n_proj, o)) for o in range(1, n_proj)]
    lapse_next = pl.pallas_call(
        functools.partial(lapse_kernel, n_proj),
        out_shape=plane, in_specs=[VMEM] * (2 + n_proj), out_specs=VMEM, name="lapse",
    )(hot, level, *costs)
    return fund_next, force_next, base_next, lapse_next, cost


def solution(mesh):
    both, proj = P("proj", "scen"), P("proj")
    paths = P(None, None, "scen")
    placed = (both,) * 4 + (proj,) * 3 + (paths, P(), P(), P(), P(), P("scen"), paths, P(), P())
    return jax.shard_map(body, mesh=mesh, in_specs=placed, out_specs=(both,) * 5, check_vma=False)
```

```python
import functools
import math

import jax
import jax.numpy as jnp
from jax import lax
from jax.experimental import pallas as pl
from jax.experimental.pallas import tpu as pltpu
from jax.sharding import PartitionSpec as P


COHORTS = 512
MONTHS_PER_YEAR = 12.0
DISCOUNT = 0.96
LAPSE_FLOOR, LAPSE_SPAN, LAPSE_SLOPE, LAPSE_PIVOT = 0.3, 2.0, 5.0, 0.4
LOG2E = 1.0 / math.log(2.0)
LANES = 128
DEPTH = 64
HIGHEST = lax.Precision.HIGHEST
F32, BF16, I32 = jnp.float32, jnp.bfloat16, jnp.int32
VMEM = pl.BlockSpec(memory_space=pltpu.VMEM)
SMEM = pl.BlockSpec(memory_space=pltpu.SMEM)
HBM = pl.BlockSpec(memory_space=pltpu.HBM)


def dot(a, b):
    return jnp.dot(a, b, preferred_element_type=F32)


def iota(shape, axis):
    return lax.broadcasted_iota(I32, shape, axis)


def split(x, parts):
    out = []
    for _ in range(parts):
        top = x.astype(BF16).astype(F32)
        out.append(top)
        x = x - top
    return out


def halves(x):
    return jnp.concatenate(split(x, 2), axis=1).astype(BF16)


def join(x):
    return x[:, :LANES] + x[:, LANES:]


def onehot(row, shape):
    return (iota(shape, 0) == row).astype(BF16)


def vmem(x):
    return pltpu.with_memory_space_constraint(x, pltpu.VMEM)


def hbm(x):
    return pltpu.with_memory_space_constraint(x, pltpu.HBM)


def limit(mebibytes):
    return pltpu.CompilerParams(vmem_limit_bytes=mebibytes << 20)


def relabel(cohort, owned, me):
    shift = owned.bit_length() - 1
    owner = jnp.bitwise_xor(lax.shift_right_logical(cohort, shift), me)
    return owner, lax.shift_left(owner, shift) + jnp.bitwise_and(cohort, owned - 1)


def project_kernel(dims, me_ref, year_ref, fee_ref, roll_ref, cohort_ref, product_ref, type_ref, mix_ref, base_ref,
                   returns_ref, fund_hbm, force_hbm, guar_hbm, lapse_hbm, *rest):
    n_proj, owned, rows, months, products, types = dims
    sends = rest[:n_proj]
    (level_ref, fund_out, force_out, guar_out, fund, force, guar, lapse, grow, table, hot, weighted, secured,
     move, gather, in_sem, out_sem) = rest[n_proj:]
    points = fund.shape[0]
    blocks = points // LANES
    combos = products * types
    sources = ((fund_hbm, fund), (guar_hbm, guar), (lapse_hbm, lapse), (force_hbm, force))
    sinks = ((fund, fund_out), (guar, guar_out), (force, force_out))

    def fetch(a):
        return pltpu.make_async_copy(*sources[a], in_sem.at[a])

    def flush(a):
        return pltpu.make_async_copy(*sinks[a], out_sem.at[a])

    for a in range(4):
        fetch(a).start()

    combo_product = lax.shift_right_logical(iota((combos, products), 0), types.bit_length() - 1)
    pick = (combo_product == iota((combos, products), 1)).astype(F32)
    mix = mix_ref[...].T
    mix = mix / jnp.sum(mix, axis=1, keepdims=True)
    mix = jnp.dot(pick, mix, precision=HIGHEST, preferred_element_type=F32)
    combo_type = jnp.bitwise_and(iota((combos, LANES), 0), types - 1)
    fee = jnp.zeros((combos, LANES), F32)
    roll = jnp.zeros((combos, LANES), F32)
    for g in range(types):
        fee = jnp.where(combo_type == g, fee_ref[g], fee)
        roll = jnp.where(combo_type == g, roll_ref[g], roll)
    keep = 1.0 - fee

    def put(column, value):
        for i, part in enumerate(split(value, 3)):
            table[i * combos:(i + 1) * combos, column * LANES:(column + 1) * LANES] = part.astype(BF16)

    for t in range(months):
        growth = 1.0 + jnp.dot(mix, returns_ref[t], precision=HIGHEST, preferred_element_type=F32)
        put(t, growth * keep)
    put(months, 1.0 + roll / MONTHS_PER_YEAR)
    level = jnp.sum(pick * base_ref[pl.ds(year_ref[0], 1), :], axis=1, keepdims=True)
    put(months + 1, jnp.broadcast_to(level, (combos, LANES)))

    combo = (product_ref[...] * types + type_ref[...]).astype(F32).T
    slot = jnp.bitwise_and(iota((LANES, 3 * combos), 1), combos - 1).astype(F32)
    for b in range(blocks):
        column = jnp.broadcast_to(combo[:, b:b + 1], (LANES, 3 * combos))
        hot[b * LANES:(b + 1) * LANES, :] = (column == slot).astype(BF16)

    owner = relabel(cohort_ref[...], owned, me_ref[0])[0]
    masks = jnp.concatenate([(owner == q).astype(F32) for q in range(n_proj)], axis=0)
    lower = (iota((LANES, LANES), 0) < iota((LANES, LANES), 1)).astype(BF16)
    before = dot(masks.astype(BF16), lower)
    count = dot(masks.astype(BF16), jnp.ones((LANES, LANES), BF16))
    size = n_proj * blocks
    r, c = iota((size, size), 0), iota((size, size), 1)
    shift = blocks.bit_length() - 1
    ahead = (lax.shift_right_logical(r, shift) == lax.shift_right_logical(c, shift)) & (c < r)
    before = before + dot(ahead.astype(BF16), count.astype(BF16))
    place = jnp.zeros((blocks, LANES), F32)
    for q in range(n_proj):
        span = slice(q * blocks, (q + 1) * blocks)
        place = place + masks[span] * before[span]

    local = jnp.bitwise_and(cohort_ref[...], owned - 1)
    place = place.astype(I32)
    kind = product_ref[...].astype(F32)
    which = iota((16, LANES), 0)
    facts = jnp.concatenate(
        [jnp.where(which == 0, kind[b:b + 1], jnp.where(which == 1, local[b:b + 1].astype(F32), 0.0)) for b in range(blocks)],
        axis=1).astype(BF16)
    for o in range(n_proj):
        mine = owner == o
        rank = jnp.where(mine, place, -1)
        label = jnp.where(mine, local, -1)
        for b in range(blocks):
            span = slice(b * LANES, (b + 1) * LANES)
            move[o * rows:(o + 1) * rows, span] = onehot(rank[b:b + 1], (rows, LANES))
            gather[o * owned:(o + 1) * owned, span] = onehot(label[b:b + 1], (owned, LANES))
    tail = dot(hot[...], table[:, months * LANES:])
    grow[...] = tail[:, :LANES]
    level_ref[...] = tail[:, LANES:]
    for a in range(2):
        fetch(a).wait()
    for t in range(0, months, 2):
        factors = dot(hot[...], table[:, t * LANES:(t + 2) * LANES])
        f = fund[...] * factors[:, :LANES]
        g = jnp.maximum(guar[...] * grow[...], f)
        f = f * factors[:, LANES:]
        guar[...] = jnp.maximum(g * grow[...], f)
        fund[...] = f
    flush(0).start()
    flush(1).start()
    for a in range(2, 4):
        fetch(a).wait()
    stay = 1.0 - lapse[...] / MONTHS_PER_YEAR
    stay = stay * stay * stay
    stay = stay * stay
    n = force[...] * (stay * stay)
    force[...] = n
    flush(2).start()
    weighted[...] = halves(n * fund[...])
    secured[...] = halves(n * guar[...])

    moved = join(dot(move[...], weighted[...]))
    summed = join(dot(gather[...], secured[...]))
    told = lax.dot_general(facts, move[...], (((1,), (1,)), ((), ())), preferred_element_type=F32)
    for o in range(n_proj):
        send = sends[o]
        send[:rows, :] = moved[o * rows:(o + 1) * rows]
        send[rows:rows + owned, :] = summed[o * owned:(o + 1) * owned]
        for b in range(rows // LANES):
            start = rows + owned + 8 * b
            first = o * rows + b * LANES
            send[start:start + 8, :] = told[:8, first:first + LANES]

    for a in range(3):
        flush(a).wait()


def hot_kernel(owned, me_ref, cohort_ref, hot_ref):
    _, label = relabel(cohort_ref[...], owned, me_ref[0])
    label = label.astype(F32).T
    slot = iota((LANES, hot_ref.shape[1]), 1).astype(F32)
    for b in range(hot_ref.shape[0] // LANES):
        column = jnp.broadcast_to(label[:, b:b + 1], slot.shape)
        hot_ref[b * LANES:(b + 1) * LANES, :] = (column == slot).astype(BF16)


def paths_kernel(shocks_ref, paths_ref):
    sources, funds, horizon, width = shocks_ref.shape
    count = sources * width
    which = iota((2 * funds, width), 0)
    for b in range(sources):
        total = jnp.zeros((funds, width), F32)
        for h in range(horizon):
            total = total + shocks_ref[b, :, h, :]
            p1, p2, p3 = split(total, 3)
            ones = jnp.where(which < 3, float(h + 1), jnp.where(which < 6, 1.0, 0.0))
            full = jnp.concatenate([p1, p1, p2, p2, p3, p1, ones], axis=0)
            start = h * count + b * width
            paths_ref[start:start + width, :] = full.T.astype(BF16)


def value_kernel(dims, vol_ref, sigma_ref, mix_ref, paths_ref, *rest):
    n_proj, owned, rows, horizon, group, step = dims
    received = rest[:n_proj]
    cost_ref, weighted, mixes, loads, spare, money = rest[n_proj:]
    funds, products = mix_ref.shape
    trials = paths_ref.shape[0] // horizon
    per = rows // LANES
    mix = mix_ref[...]
    mix = mix / jnp.sum(mix, axis=0, keepdims=True)
    tops, lows = [], []
    labels = []
    for o in range(n_proj):
        weighted[o * rows:(o + 1) * rows, :] = halves(received[o][:rows, :])
        for b in range(per):
            start = rows + owned + 8 * b
            facts = received[o][start:start + 8, :]
            hot = (jnp.broadcast_to(facts[0:1], (products, LANES)).astype(I32) == iota((products, LANES), 0)).astype(F32)
            share = lax.dot_general(mix, hot, (((1,), (0,)), ((), ())), precision=HIGHEST, preferred_element_type=F32)
            top, low = split(share, 2)
            tops.append(top)
            lows.append(low)
            labels.append(facts[1:2].astype(I32))
    spans = n_proj * per
    for b in range(spans):
        mixes[0, b] = tops[b]
        mixes[1, b] = lows[b]
    vol = jnp.zeros((funds, LANES), F32)
    for f in range(funds):
        vol = jnp.where(iota((funds, LANES), 0) == f, vol_ref[f], vol)
    sigma = sigma_ref[...]
    scale = sigma * LOG2E
    slope = -0.5 * sigma * sigma * LOG2E
    which = iota((funds, LANES), 0)

    def prepare(i, loads):
        first = i * group
        sides = []
        for part in range(2):
            wide = []
            for b in range(spans):
                share = mixes[part, b]
                wide.append(jnp.concatenate(
                    [jnp.where(labels[b] == first + c, share, 0.0) for c in range(group)], axis=0).astype(BF16))
            sides.append(jnp.concatenate(wide, axis=1))
        sums = join(dot(sides[0], weighted[...]) + dot(sides[1], weighted[...]))
        span = pl.ds(pl.multiple_of(rows + first, 8), group)
        secured = received[0][span, :]
        for o in range(1, n_proj):
            secured = secured + received[o][span, :]
        for c in range(group):
            part = sums[c * funds:(c + 1) * funds]
            inverse = 1.0 / jnp.sum(part, axis=0, keepdims=True)
            load = part * inverse * vol
            ratio = secured[c:c + 1] * inverse
            money[pl.ds(first + c, 1), :] = ratio
            spread = jnp.sum(load * load, axis=0, keepdims=True)
            w1, w2, w3 = split(load * scale, 3)
            d = split(slope * spread, 3) + split(-LOG2E * jnp.log(ratio), 3)
            extra = jnp.zeros((funds, LANES), F32)
            for k in range(6):
                extra = jnp.where(which == k, d[k], extra)
            full = jnp.concatenate([w1, w2, w1, w2, w1, w3, extra, jnp.zeros_like(extra)], axis=0)
            loads[:, c * LANES:(c + 1) * LANES] = full.astype(BF16)

    def value(i, loads):
        right = loads[...]
        total = None
        for h in range(horizon):
            reach = jnp.zeros((8, group * LANES), F32)
            for s in range(trials // step):
                left = paths_ref[h * trials + s * step:h * trials + (s + 1) * step, :]
                kept = jnp.exp2(jnp.minimum(dot(left, right), 0.0))
                reach = reach + jnp.sum(kept.reshape(step // 8, 8, group * LANES), axis=0)
            part = (float(trials) - jnp.sum(reach, axis=0, keepdims=True)) * (DISCOUNT ** (h + 1) / trials)
            total = part if total is None else total + part
        for c in range(group):
            row = pl.ds(i * group + c, 1)
            cost_ref[row, :] = total[:, c * LANES:(c + 1) * LANES] * money[row, :]

    turns = owned // group
    prepare(0, loads)

    def pair(j, _):
        prepare(2 * j + 1, spare)
        value(2 * j, loads)
        prepare(jnp.minimum(2 * j + 2, turns - 1), loads)
        value(2 * j + 1, spare)
        return 0

    lax.fori_loop(0, turns // 2, pair, 0)


def lapse_kernel(n_proj, hot_ref, level_ref, *rest):
    costs, (out_hbm, out, sem) = rest[:n_proj], rest[n_proj:]
    factors = jnp.concatenate(
        [halves(LAPSE_FLOOR + LAPSE_SPAN * jax.nn.sigmoid(LAPSE_SLOPE * (LAPSE_PIVOT - cost[...]))) for cost in costs],
        axis=0)
    chunk = 2 * LANES

    def flush(i):
        span = pl.ds(i * chunk, chunk)
        return pltpu.make_async_copy(out.at[span], out_hbm.at[span], sem.at[i])

    chunks = out.shape[0] // chunk
    for i in range(chunks):
        span = slice(i * chunk, (i + 1) * chunk)
        out[span, :] = level_ref[span, :] * join(dot(hot_ref[span, :], factors))
        flush(i).start()
    for i in range(chunks):
        flush(i).wait()


def exchange(x, axis, offset):
    return lax.ppermute(x, axis, flips(lax.axis_size(axis), offset))


def flips(n, offset):
    return [(i, i ^ offset) for i in range(n)]


def body(fund_value, in_force, guarantee_base, lapse_rate, cohort, product, guarantee_type, returns, mix_table,
         fee_table, rollup_table, fund_vol, closing_sigma_figure, shocks, base_table, year_index):
    n_proj, n_scen = lax.axis_size("proj"), lax.axis_size("scen")
    points, width = fund_value.shape
    funds, months, _ = returns.shape
    horizon = shocks.shape[1]
    products, types = mix_table.shape[0], fee_table.shape[0]
    owned = COHORTS // n_proj
    rows = -(-points // n_proj // LANES) * LANES
    message = rows + owned + 8 * (rows // LANES)
    blocks = points // LANES
    me = lax.axis_index("proj").astype(I32).reshape(1)
    plane = jax.ShapeDtypeStruct((points, width), F32)
    labels = cohort.reshape(blocks, LANES)
    mix = mix_table.T

    sheets = jnp.concatenate([shocks[None], exchange(shocks[None], "scen", 1)], axis=0)
    outs = pl.pallas_call(
        functools.partial(project_kernel, (n_proj, owned, rows, months, products, types)),
        out_shape=[pltpu.VMEM((message, width), F32)] * n_proj + [pltpu.VMEM((points, width), F32)] + [plane] * 3,
        in_specs=[SMEM] * 4 + [VMEM] * 6 + [HBM] * 4,
        out_specs=[VMEM] * (n_proj + 1) + [HBM] * 3,
        scratch_shapes=[pltpu.VMEM((points, width), F32)] * 5 + [
            pltpu.VMEM((3 * products * types, (months + 2) * LANES), BF16),
            pltpu.VMEM((points, 3 * products * types), BF16),
            pltpu.VMEM((points, 2 * width), BF16),
            pltpu.VMEM((points, 2 * width), BF16),
            pltpu.VMEM((n_proj * rows, points), BF16),
            pltpu.VMEM((COHORTS, points), BF16),
            pltpu.SemaphoreType.DMA((4,)),
            pltpu.SemaphoreType.DMA((3,)),
        ],
        compiler_params=limit(24), name="project",
    )(me, year_index, hbm(fee_table), hbm(rollup_table), hbm(labels), hbm(product.reshape(blocks, LANES)),
      hbm(guarantee_type.reshape(blocks, LANES)), hbm(mix), hbm(base_table), hbm(returns.transpose(1, 0, 2)),
      hbm(fund_value), hbm(in_force), hbm(guarantee_base), hbm(lapse_rate))
    sends, (level, fund_next, force_next, base_next) = outs[:n_proj], outs[n_proj:]

    sheets, *sends = lax.optimization_barrier((sheets, *sends))
    received = [sends[0]] + [vmem(exchange(sends[o], "proj", o)) for o in range(1, n_proj)]

    offset = 2
    while offset < n_scen:
        if 2 * offset >= n_scen:
            sheets, labels = lax.optimization_barrier((sheets, labels))
        sheets = jnp.concatenate([sheets, exchange(sheets, "scen", offset)], axis=0)
        offset *= 2
    trials = n_scen * shocks.shape[2]

    hot = pl.pallas_call(
        functools.partial(hot_kernel, owned),
        out_shape=pltpu.VMEM((points, COHORTS), BF16),
        in_specs=[SMEM, VMEM], out_specs=VMEM, compiler_params=limit(8), name="cohort_hot",
    )(me, labels)
    left = pl.pallas_call(
        paths_kernel,
        out_shape=pltpu.VMEM((horizon * trials, DEPTH), BF16),
        in_specs=[VMEM], out_specs=VMEM, compiler_params=limit(8), name="paths",
    )(vmem(sheets))
    left, hot = lax.optimization_barrier((left, hot))

    group = 16
    cost = pl.pallas_call(
        functools.partial(value_kernel, (n_proj, owned, rows, horizon, group, 64)),
        out_shape=pltpu.VMEM((owned, width), F32),
        in_specs=[SMEM] + [VMEM] * (3 + n_proj), out_specs=VMEM,
        scratch_shapes=[
            pltpu.VMEM((n_proj * rows, 2 * width), BF16),
            pltpu.VMEM((2, n_proj * rows // LANES, funds, LANES), F32),
            pltpu.VMEM((DEPTH, group * LANES), BF16),
            pltpu.VMEM((DEPTH, group * LANES), BF16),
            pltpu.VMEM((owned, width), F32),
        ],
        compiler_params=limit(24), name="value",
    )(hbm(fund_vol), hbm(closing_sigma_figure.reshape(1, width)), hbm(mix), left, *received)

    costs = [cost] + [vmem(lax.ppermute(cost, "proj", flips(n_proj, o))) for o in range(1, n_proj)]
    lapse_next = pl.pallas_call(
        functools.partial(lapse_kernel, n_proj),
        out_shape=plane, in_specs=[VMEM] * (2 + n_proj), out_specs=HBM,
        scratch_shapes=[pltpu.VMEM((points, width), F32), pltpu.SemaphoreType.DMA((points // (2 * LANES),))],
        compiler_params=limit(16), name="lapse",
    )(hot, level, *costs)
    return fund_next, force_next, base_next, lapse_next, cost


def solution(mesh):
    both, proj = P("proj", "scen"), P("proj")
    paths = P(None, None, "scen")
    placed = (both,) * 4 + (proj,) * 3 + (paths, P(), P(), P(), P(), P("scen"), paths, P(), P())
    return jax.shard_map(body, mesh=mesh, in_specs=placed, out_specs=(both,) * 5, check_vma=False)
```

```python
import functools
import math

import jax
import jax.numpy as jnp
from jax import lax
from jax.experimental import pallas as pl
from jax.experimental.pallas import tpu as pltpu
from jax.sharding import PartitionSpec as P


COHORTS = 512
MONTHS_PER_YEAR = 12.0
DISCOUNT = 0.96
LAPSE_FLOOR, LAPSE_SPAN, LAPSE_SLOPE, LAPSE_PIVOT = 0.3, 2.0, 5.0, 0.4
LOG2E = 1.0 / math.log(2.0)
LANES = 128
DEPTH = 64
HIGHEST = lax.Precision.HIGHEST
F32, BF16, I32 = jnp.float32, jnp.bfloat16, jnp.int32
VMEM = pl.BlockSpec(memory_space=pltpu.VMEM)
HBM = pl.BlockSpec(memory_space=pltpu.HBM)


def dot(a, b):
    return jnp.dot(a, b, preferred_element_type=F32)


def iota(shape, axis):
    return lax.broadcasted_iota(I32, shape, axis)


def split(x, parts):
    out = []
    for _ in range(parts):
        top = x.astype(BF16).astype(F32)
        out.append(top)
        x = x - top
    return out


def halves(x):
    return jnp.concatenate(split(x, 2), axis=1).astype(BF16)


def join(x):
    return x[:, :LANES] + x[:, LANES:]


def onehot(row, ramp):
    return jnp.where(ramp == row, 1.0, 0.0).astype(BF16)


def vmem(x):
    return pltpu.with_memory_space_constraint(x, pltpu.VMEM)


def hbm(x):
    return pltpu.with_memory_space_constraint(x, pltpu.HBM)


def limit(mebibytes):
    return pltpu.CompilerParams(vmem_limit_bytes=mebibytes << 20)


def relabel(cohort, owned, me):
    shift = owned.bit_length() - 1
    owner = jnp.bitwise_xor(lax.shift_right_logical(cohort, shift), me)
    return owner, lax.shift_left(owner, shift) + jnp.bitwise_and(cohort, owned - 1)


def project_kernel(dims, *refs):
    n_proj, owned, rows = dims
    small, big = refs[:7], refs[7:11]
    sends, refs = refs[11:11 + n_proj], refs[11 + n_proj:]
    results, local_small, planes = refs[:3], refs[3:10], refs[10:14]
    table, hot, weighted, secured, move, gather, ramp, small_sem, in_sem = refs[14:]
    cohort_ref, product_ref, type_ref, fee_ref, roll_ref, mix_ref, returns_ref = local_small
    fund, force, guar, lapse = planes
    points = fund.shape[0]
    blocks = points // LANES
    months = returns_ref.shape[0]
    products, types = mix_ref.shape[1], fee_ref.shape[1]
    combos = products * types

    reads = [pltpu.make_async_copy(small[i], local_small[i], small_sem.at[i]) for i in range(7)]
    loads = [pltpu.make_async_copy(big[i], planes[i], in_sem.at[i]) for i in range(4)]
    for copy in reads + loads:
        copy.start()
    ramp[...] = iota(ramp.shape, 0).astype(F32)
    for copy in reads:
        copy.wait()

    cohort = cohort_ref[...]
    owner = relabel(cohort, owned, lax.axis_index("proj"))[0]
    local = jnp.bitwise_and(cohort, owned - 1).astype(F32)
    masks = jnp.concatenate([(owner == q).astype(F32) for q in range(n_proj)], axis=0)
    lower = (iota((LANES, LANES), 0) < iota((LANES, LANES), 1)).astype(BF16)
    before = dot(masks.astype(BF16), lower)
    count = dot(masks.astype(BF16), jnp.ones((LANES, LANES), BF16))
    size = n_proj * blocks
    r, c = iota((size, size), 0), iota((size, size), 1)
    shift = blocks.bit_length() - 1
    ahead = (lax.shift_right_logical(r, shift) == lax.shift_right_logical(c, shift)) & (c < r)
    before = before + dot(ahead.astype(BF16), count.astype(BF16))

    mix = mix_ref[...].T
    mix = mix / jnp.sum(mix, axis=1, keepdims=True)
    shares = [jnp.broadcast_to(mix[:, f:f + 1], (products, LANES)) for f in range(mix.shape[1])]
    wide = (products, LANES)
    keeps = [jnp.broadcast_to(1.0 - fee_ref[:, g:g + 1], wide) for g in range(types)]
    rolls = [jnp.broadcast_to(1.0 + roll_ref[:, g:g + 1] / MONTHS_PER_YEAR, wide) for g in range(types)]
    held = [jnp.ones(wide, F32)] * types
    best = [jnp.zeros(wide, F32)] * types
    rolled = [jnp.ones(wide, F32)] * types
    for t in range(months):
        month = returns_ref[t]
        growth = 1.0 + sum(share * month[f:f + 1] for f, share in enumerate(shares))
        for g in range(types):
            held[g] = held[g] * growth * keeps[g]
            best[g] = jnp.maximum(best[g] * rolls[g], held[g])
            rolled[g] = rolled[g] * rolls[g]
    for column, value in enumerate((held, best, rolled)):
        for i, part in enumerate(split(jnp.concatenate(value, axis=0), 3)):
            table[i * combos:(i + 1) * combos, column * LANES:(column + 1) * LANES] = part.astype(BF16)

    combo = (type_ref[...] * products + product_ref[...]).astype(F32).T
    slot = iota((LANES, 3 * combos), 1)
    slot = (slot - combos * ((slot >= combos).astype(I32) + (slot >= 2 * combos).astype(I32))).astype(F32)
    for b in range(blocks):
        column = jnp.broadcast_to(combo[:, b:b + 1], slot.shape)
        hot[b * LANES:(b + 1) * LANES, :] = onehot(column, slot)

    for o in range(n_proj):
        mine = masks[o * blocks:(o + 1) * blocks] > 0.0
        rank = jnp.where(mine, before[o * blocks:(o + 1) * blocks], -1.0)
        label = jnp.where(mine, local, -1.0)
        for b in range(blocks):
            span = slice(b * LANES, (b + 1) * LANES)
            move[o * rows:(o + 1) * rows, span] = onehot(rank[b:b + 1], ramp[:rows, :])
            gather[o * owned:(o + 1) * owned, span] = onehot(label[b:b + 1], ramp[:owned, :])
    kind = product_ref[...].astype(F32)
    which = iota((16, LANES), 0)
    facts = jnp.concatenate(
        [jnp.where(which == 0, kind[b:b + 1], jnp.where(which == 1, local[b:b + 1], 0.0)) for b in range(blocks)],
        axis=1).astype(BF16)
    told = lax.dot_general(facts, move[...], (((1,), (1,)), ((), ())), preferred_element_type=F32)

    for copy in loads:
        copy.wait()
    factors = dot(hot[...], table[...])
    stay = 1.0 - lapse[...] / MONTHS_PER_YEAR
    stay = stay * stay * stay
    stay = stay * stay
    n = force[...] * (stay * stay)
    f = fund[...]
    g = jnp.maximum(guar[...] * factors[:, 2 * LANES:3 * LANES], f * factors[:, LANES:2 * LANES])
    f = f * factors[:, :LANES]
    for result, value in zip(results, (f, n, g)):
        result[...] = value
    weighted[...] = halves(n * f)
    secured[...] = halves(n * g)
    moved = join(dot(move[...], weighted[...]))
    summed = join(dot(gather[...], secured[...]))
    for o in range(n_proj):
        send = sends[o]
        send[:rows, :] = moved[o * rows:(o + 1) * rows]
        send[rows:rows + owned, :] = summed[o * owned:(o + 1) * owned]
        for b in range(rows // LANES):
            start = rows + owned + 2 * b
            first = o * rows + b * LANES
            send[start:start + 2, :] = told[:2, first:first + LANES]


def hot_kernel(owned, year_ref, cohort_ref, product_ref, base_ref, *refs):
    planes, (hot_ref, level_ref), results, sem = refs[:3], refs[3:5], refs[5:8], refs[8]
    stores = [pltpu.make_async_copy(planes[i], results[i], sem.at[i]) for i in range(3)]
    for copy in stores:
        copy.start()
    _, label = relabel(cohort_ref[...], owned, lax.axis_index("proj"))
    label = label.astype(F32).T
    product = product_ref[...].astype(F32).T
    slot = iota((LANES, hot_ref.shape[1]), 1).astype(F32)
    rates = base_ref[pl.ds(year_ref[0], 1), :]
    for b in range(hot_ref.shape[0] // LANES):
        span = slice(b * LANES, (b + 1) * LANES)
        hot_ref[span, :] = onehot(jnp.broadcast_to(label[:, b:b + 1], slot.shape), slot)
        kind = jnp.broadcast_to(product[:, b:b + 1], (LANES, rates.shape[1]))
        rate = jnp.sum(jnp.where(kind == slot[:, :rates.shape[1]], rates, 0.0), axis=1, keepdims=True)
        level_ref[span, :] = jnp.broadcast_to(rate, (LANES, LANES))
    for copy in stores:
        copy.wait()


def paths_kernel(shocks_ref, paths_ref):
    sources, funds, horizon, width = shocks_ref.shape
    count = sources * width
    which = iota((2 * funds, width), 0)
    for b in range(sources):
        total = jnp.zeros((funds, width), F32)
        for h in range(horizon):
            total = total + shocks_ref[b, :, h, :]
            p1, p2, p3 = split(total, 3)
            ones = jnp.where(which < 3, float(h + 1), jnp.where(which < 6, 1.0, 0.0))
            full = jnp.concatenate([p1, p1, p2, p2, p3, p1, ones], axis=0)
            start = h * count + b * width
            paths_ref[start:start + width, :] = full.T.astype(BF16)


def value_kernel(dims, vol_ref, sigma_ref, mix_ref, paths_ref, *rest):
    n_proj, owned, rows, horizon, group, step = dims
    received = rest[:n_proj]
    cost_ref, weighted, mixes, loads, spare, money = rest[n_proj:]
    funds, products = mix_ref.shape
    trials = paths_ref.shape[0] // horizon
    per = rows // LANES
    mix = mix_ref[...]
    mix = mix / jnp.sum(mix, axis=0, keepdims=True)
    tops, lows = [], []
    labels = []
    for o in range(n_proj):
        weighted[o * rows:(o + 1) * rows, :] = halves(received[o][:rows, :])
        for b in range(per):
            start = rows + owned + 2 * b
            facts = received[o][start:start + 2, :]
            hot = (jnp.broadcast_to(facts[0:1], (products, LANES)).astype(I32) == iota((products, LANES), 0)).astype(F32)
            share = lax.dot_general(mix, hot, (((1,), (0,)), ((), ())), precision=HIGHEST, preferred_element_type=F32)
            top, low = split(share, 2)
            tops.append(top)
            lows.append(low)
            labels.append(facts[1:2].astype(I32))
    spans = n_proj * per
    for b in range(spans):
        mixes[0, b] = tops[b]
        mixes[1, b] = lows[b]
    same = (iota((funds, funds), 0) == iota((funds, funds), 1)).astype(F32)
    vol = jnp.broadcast_to(jnp.sum(same * vol_ref[...], axis=1, keepdims=True), (funds, LANES))
    sigma = sigma_ref[...]
    scale = sigma * LOG2E
    slope = -0.5 * sigma * sigma * LOG2E
    which = iota((funds, LANES), 0)

    def prepare(i, loads):
        first = i * group
        sides = []
        for part in range(2):
            wide = []
            for b in range(spans):
                share = mixes[part, b]
                wide.append(jnp.concatenate(
                    [jnp.where(labels[b] == first + c, share, 0.0) for c in range(group)], axis=0).astype(BF16))
            sides.append(jnp.concatenate(wide, axis=1))
        sums = join(dot(sides[0], weighted[...]) + dot(sides[1], weighted[...]))
        span = pl.ds(pl.multiple_of(rows + first, 8), group)
        secured = received[0][span, :]
        for o in range(1, n_proj):
            secured = secured + received[o][span, :]
        for c in range(group):
            part = sums[c * funds:(c + 1) * funds]
            inverse = 1.0 / jnp.sum(part, axis=0, keepdims=True)
            load = part * inverse * vol
            ratio = secured[c:c + 1] * inverse
            money[pl.ds(first + c, 1), :] = ratio
            spread = jnp.sum(load * load, axis=0, keepdims=True)
            w1, w2, w3 = split(load * scale, 3)
            d = split(slope * spread, 3) + split(-LOG2E * jnp.log(ratio), 3)
            extra = jnp.zeros((funds, LANES), F32)
            for k in range(6):
                extra = jnp.where(which == k, d[k], extra)
            full = jnp.concatenate([w1, w2, w1, w2, w1, w3, extra, jnp.zeros_like(extra)], axis=0)
            loads[:, c * LANES:(c + 1) * LANES] = full.astype(BF16)

    def value(i, loads):
        right = loads[...]
        total = None
        for h in range(horizon):
            reach = jnp.zeros((8, group * LANES), F32)
            for s in range(trials // step):
                left = paths_ref[h * trials + s * step:h * trials + (s + 1) * step, :]
                kept = jnp.exp2(jnp.minimum(dot(left, right), 0.0))
                reach = reach + jnp.sum(kept.reshape(step // 8, 8, group * LANES), axis=0)
            part = (float(trials) - jnp.sum(reach, axis=0, keepdims=True)) * (DISCOUNT ** (h + 1) / trials)
            total = part if total is None else total + part
        for c in range(group):
            row = pl.ds(i * group + c, 1)
            cost_ref[row, :] = total[:, c * LANES:(c + 1) * LANES] * money[row, :]

    turns = owned // group
    prepare(0, loads)

    def pair(j, _):
        prepare(2 * j + 1, spare)
        value(2 * j, loads)
        prepare(jnp.minimum(2 * j + 2, turns - 1), loads)
        value(2 * j + 1, spare)
        return 0

    lax.fori_loop(0, turns // 2, pair, 0)


def lapse_kernel(n_proj, hot_ref, level_ref, *rest):
    costs, (out_hbm, out, sem) = rest[:n_proj], rest[n_proj:]
    factors = jnp.concatenate(
        [halves(LAPSE_FLOOR + LAPSE_SPAN * jax.nn.sigmoid(LAPSE_SLOPE * (LAPSE_PIVOT - cost[...]))) for cost in costs],
        axis=0)
    chunk = 2 * LANES

    def flush(i):
        span = pl.ds(i * chunk, chunk)
        return pltpu.make_async_copy(out.at[span], out_hbm.at[span], sem.at[i])

    chunks = out.shape[0] // chunk
    for i in range(chunks):
        span = slice(i * chunk, (i + 1) * chunk)
        out[span, :] = level_ref[span, :] * join(dot(hot_ref[span, :], factors))
        flush(i).start()
    for i in range(chunks):
        flush(i).wait()


def exchange(x, axis, offset):
    return lax.ppermute(x, axis, flips(lax.axis_size(axis), offset))


def flips(n, offset):
    return [(i, i ^ offset) for i in range(n)]


def body(fund_value, in_force, guarantee_base, lapse_rate, cohort, product, guarantee_type, returns, mix_table,
         fee_table, rollup_table, fund_vol, closing_sigma_figure, shocks, base_table, year_index):
    n_proj, n_scen = lax.axis_size("proj"), lax.axis_size("scen")
    points, width = fund_value.shape
    funds, _, _ = returns.shape
    horizon = shocks.shape[1]
    products, types = mix_table.shape[0], fee_table.shape[0]
    owned = COHORTS // n_proj
    rows = -(-points // n_proj // LANES) * LANES
    message = rows + owned + 8 * -(-2 * (rows // LANES) // 8)
    blocks = points // LANES
    plane = jax.ShapeDtypeStruct((points, width), F32)
    labels = cohort.reshape(blocks, LANES)
    mix = mix_table.T

    sheets = jnp.concatenate([shocks[None], exchange(shocks[None], "scen", 1)], axis=0)
    kinds = product.reshape(blocks, LANES)
    small = [labels, kinds, guarantee_type.reshape(blocks, LANES), fee_table.reshape(1, types),
             rollup_table.reshape(1, types), mix, returns.transpose(1, 0, 2)]
    big = [fund_value, in_force, guarantee_base, lapse_rate]
    outs = pl.pallas_call(
        functools.partial(project_kernel, (n_proj, owned, rows)),
        out_shape=[pltpu.VMEM((message, width), F32)] * n_proj + [pltpu.VMEM((points, width), F32)] * 3,
        in_specs=[HBM] * 11,
        out_specs=[VMEM] * (n_proj + 3),
        scratch_shapes=[pltpu.VMEM(x.shape, x.dtype) for x in small + big] + [
            pltpu.VMEM((3 * products * types, 3 * LANES), BF16),
            pltpu.VMEM((points, 3 * products * types), BF16),
            pltpu.VMEM((points, 2 * width), BF16),
            pltpu.VMEM((points, 2 * width), BF16),
            pltpu.VMEM((n_proj * rows, points), BF16),
            pltpu.VMEM((COHORTS, points), BF16),
            pltpu.VMEM((max(rows, owned), LANES), F32),
            pltpu.SemaphoreType.DMA((7,)),
            pltpu.SemaphoreType.DMA((4,)),
        ],
        compiler_params=limit(24), name="project",
    )(*[hbm(x) for x in small + big])
    sends, planes = outs[:n_proj], outs[n_proj:]

    sheets, *sends = lax.optimization_barrier((sheets, *sends))
    received = [sends[0]] + [vmem(exchange(sends[o], "proj", o)) for o in range(1, n_proj)]

    offset = 2
    while offset < n_scen:
        if 2 * offset >= n_scen:
            sheets, labels, year_index = lax.optimization_barrier((sheets, labels, year_index))
        sheets = jnp.concatenate([sheets, exchange(sheets, "scen", offset)], axis=0)
        offset *= 2
    trials = n_scen * shocks.shape[2]

    hot, level, fund_next, force_next, base_next = pl.pallas_call(
        functools.partial(hot_kernel, owned),
        out_shape=[pltpu.VMEM((points, COHORTS), BF16), pltpu.VMEM((points, width), F32)] + [plane] * 3,
        in_specs=[pl.BlockSpec(memory_space=pltpu.SMEM)] + [VMEM] * 6, out_specs=[VMEM] * 2 + [HBM] * 3,
        scratch_shapes=[pltpu.SemaphoreType.DMA((3,))],
        compiler_params=limit(8), name="cohort_hot",
    )(year_index, labels, kinds, base_table, *planes)
    left = pl.pallas_call(
        paths_kernel,
        out_shape=pltpu.VMEM((horizon * trials, DEPTH), BF16),
        in_specs=[VMEM], out_specs=VMEM, compiler_params=limit(8), name="paths",
    )(vmem(sheets))
    left, hot = lax.optimization_barrier((left, hot))

    group = 16
    cost = pl.pallas_call(
        functools.partial(value_kernel, (n_proj, owned, rows, horizon, group, 64)),
        out_shape=pltpu.VMEM((owned, width), F32),
        in_specs=[VMEM] * (4 + n_proj), out_specs=VMEM,
        scratch_shapes=[
            pltpu.VMEM((n_proj * rows, 2 * width), BF16),
            pltpu.VMEM((2, n_proj * rows // LANES, funds, LANES), F32),
            pltpu.VMEM((DEPTH, group * LANES), BF16),
            pltpu.VMEM((DEPTH, group * LANES), BF16),
            pltpu.VMEM((owned, width), F32),
        ],
        compiler_params=limit(24), name="value",
    )(hbm(fund_vol.reshape(1, funds)), hbm(closing_sigma_figure.reshape(1, width)), hbm(mix), left, *received)

    costs = [cost]
    for o in range(1, n_proj):
        near = o % 2 and o > 1
        costs.append(exchange(costs[o - 1] if near else cost, "proj", 1 if near else o))
    costs = [cost] + [vmem(x) for x in costs[1:]]
    lapse_next = pl.pallas_call(
        functools.partial(lapse_kernel, n_proj),
        out_shape=plane, in_specs=[VMEM] * (2 + n_proj), out_specs=HBM,
        scratch_shapes=[pltpu.VMEM((points, width), F32), pltpu.SemaphoreType.DMA((points // (2 * LANES),))],
        compiler_params=limit(16), name="lapse",
    )(hot, level, *costs)
    return fund_next, force_next, base_next, lapse_next, cost


def solution(mesh):
    both, proj = P("proj", "scen"), P("proj")
    paths = P(None, None, "scen")
    placed = (both,) * 4 + (proj,) * 3 + (paths, P(), P(), P(), P(), P("scen"), paths, P(), P())
    return jax.shard_map(body, mesh=mesh, in_specs=placed, out_specs=(both,) * 5, check_vma=False)
```

```python
import functools
import math

import jax
import jax.numpy as jnp
from jax import lax
from jax.experimental import pallas as pl
from jax.experimental.pallas import tpu as pltpu
from jax.sharding import PartitionSpec as P


COHORTS = 512
MONTHS_PER_YEAR = 12.0
DISCOUNT = 0.96
LAPSE_FLOOR, LAPSE_SPAN, LAPSE_SLOPE, LAPSE_PIVOT = 0.3, 2.0, 5.0, 0.4
LOG2E = 1.0 / math.log(2.0)
LANES = 128
DEPTH = 64
HIGHEST = lax.Precision.HIGHEST
F32, BF16, I32 = jnp.float32, jnp.bfloat16, jnp.int32
VMEM = pl.BlockSpec(memory_space=pltpu.VMEM)
HBM = pl.BlockSpec(memory_space=pltpu.HBM)


def dot(a, b):
    return jnp.dot(a, b, preferred_element_type=F32)


def iota(shape, axis):
    return lax.broadcasted_iota(I32, shape, axis)


def split(x, parts):
    out = []
    for _ in range(parts):
        top = x.astype(BF16).astype(F32)
        out.append(top)
        x = x - top
    return out


def halves(x):
    return jnp.concatenate(split(x, 2), axis=1).astype(BF16)


def join(x):
    return x[:, :LANES] + x[:, LANES:]


def onehot(row, ramp):
    return jnp.where(ramp == row, 1.0, 0.0).astype(BF16)


def vmem(x):
    return pltpu.with_memory_space_constraint(x, pltpu.VMEM)


def hbm(x):
    return pltpu.with_memory_space_constraint(x, pltpu.HBM)


def limit(mebibytes):
    return pltpu.CompilerParams(vmem_limit_bytes=mebibytes << 20)


def relabel(cohort, owned, me):
    shift = owned.bit_length() - 1
    owner = jnp.bitwise_xor(lax.shift_right_logical(cohort, shift), me)
    return owner, lax.shift_left(owner, shift) + jnp.bitwise_and(cohort, owned - 1)


def project_kernel(dims, *refs):
    n_proj, owned, rows = dims
    small, big = refs[:7], refs[7:11]
    sends, refs = refs[11:11 + n_proj], refs[11 + n_proj:]
    results, local_small, planes = refs[:3], refs[3:10], refs[10:14]
    table, hot, weighted, secured, move, gather, ramp, small_sem, in_sem = refs[14:]
    cohort_ref, product_ref, type_ref, fee_ref, roll_ref, mix_ref, returns_ref = local_small
    fund, force, guar, lapse = planes
    points = fund.shape[0]
    blocks = points // LANES
    months = returns_ref.shape[0]
    products, types = mix_ref.shape[1], fee_ref.shape[1]
    combos = products * types

    reads = [pltpu.make_async_copy(small[i], local_small[i], small_sem.at[i]) for i in range(7)]
    loads = [pltpu.make_async_copy(big[i], planes[i], in_sem.at[i]) for i in range(4)]
    for copy in reads + loads:
        copy.start()
    ramp[...] = iota(ramp.shape, 0).astype(F32)
    for copy in reads:
        copy.wait()

    cohort = cohort_ref[...]
    owner = relabel(cohort, owned, lax.axis_index("proj"))[0]
    local = jnp.bitwise_and(cohort, owned - 1).astype(F32)
    masks = jnp.concatenate([(owner == q).astype(F32) for q in range(n_proj)], axis=0)
    lower = (iota((LANES, LANES), 0) < iota((LANES, LANES), 1)).astype(BF16)
    before = dot(masks.astype(BF16), lower)
    count = dot(masks.astype(BF16), jnp.ones((LANES, LANES), BF16))
    size = n_proj * blocks
    r, c = iota((size, size), 0), iota((size, size), 1)
    shift = blocks.bit_length() - 1
    ahead = (lax.shift_right_logical(r, shift) == lax.shift_right_logical(c, shift)) & (c < r)
    before = before + dot(ahead.astype(BF16), count.astype(BF16))

    mix = mix_ref[...].T
    mix = mix / jnp.sum(mix, axis=1, keepdims=True)
    shares = [jnp.broadcast_to(mix[:, f:f + 1], (products, LANES)) for f in range(mix.shape[1])]
    wide = (products, LANES)
    keeps = [jnp.broadcast_to(1.0 - fee_ref[:, g:g + 1], wide) for g in range(types)]
    rolls = [jnp.broadcast_to(1.0 + roll_ref[:, g:g + 1] / MONTHS_PER_YEAR, wide) for g in range(types)]
    held = [jnp.ones(wide, F32)] * types
    best = [jnp.zeros(wide, F32)] * types
    rolled = [jnp.ones(wide, F32)] * types
    for t in range(months):
        month = returns_ref[t]
        growth = 1.0 + sum(share * month[f:f + 1] for f, share in enumerate(shares))
        for g in range(types):
            held[g] = held[g] * growth * keeps[g]
            best[g] = jnp.maximum(best[g] * rolls[g], held[g])
            rolled[g] = rolled[g] * rolls[g]
    for column, value in enumerate((held, best, rolled)):
        for i, part in enumerate(split(jnp.concatenate(value, axis=0), 3)):
            table[i * combos:(i + 1) * combos, column * LANES:(column + 1) * LANES] = part.astype(BF16)

    combo = (type_ref[...] * products + product_ref[...]).astype(F32).T
    slot = iota((LANES, 3 * combos), 1)
    slot = (slot - combos * ((slot >= combos).astype(I32) + (slot >= 2 * combos).astype(I32))).astype(F32)
    for b in range(blocks):
        column = jnp.broadcast_to(combo[:, b:b + 1], slot.shape)
        hot[b * LANES:(b + 1) * LANES, :] = onehot(column, slot)

    def arrange(o):
        mine = masks[o * blocks:(o + 1) * blocks] > 0.0
        rank = jnp.where(mine, before[o * blocks:(o + 1) * blocks], -1.0)
        for b in range(blocks):
            move[o * rows:(o + 1) * rows, b * LANES:(b + 1) * LANES] = onehot(rank[b:b + 1], ramp[:rows, :])

    for o in range(n_proj):
        label = jnp.where(masks[o * blocks:(o + 1) * blocks] > 0.0, local, -1.0)
        for b in range(blocks):
            span = slice(b * LANES, (b + 1) * LANES)
            gather[o * owned:(o + 1) * owned, span] = onehot(label[b:b + 1], ramp[:owned, :])
    for o in range(n_proj // 2):
        arrange(o)
    kind = product_ref[...].astype(F32)
    which = iota((16, LANES), 0)
    facts = jnp.concatenate(
        [jnp.where(which == 0, kind[b:b + 1], jnp.where(which == 1, local[b:b + 1], 0.0)) for b in range(blocks)],
        axis=1).astype(BF16)

    for copy in loads:
        copy.wait()
    factors = dot(hot[...], table[...])
    stay = 1.0 - lapse[...] / MONTHS_PER_YEAR
    stay = stay * stay * stay
    stay = stay * stay
    n = force[...] * (stay * stay)
    f = fund[...]
    g = jnp.maximum(guar[...] * factors[:, 2 * LANES:3 * LANES], f * factors[:, LANES:2 * LANES])
    f = f * factors[:, :LANES]
    for result, value in zip(results, (f, n, g)):
        result[...] = value
    weighted[...] = halves(n * f)
    secured[...] = halves(n * g)
    summed = join(dot(gather[...], secured[...]))
    for first in (0, n_proj // 2):
        span = slice(first * rows, (first + n_proj // 2) * rows)
        moved = join(dot(move[span, :], weighted[...]))
        told = lax.dot_general(facts, move[span, :], (((1,), (1,)), ((), ())), preferred_element_type=F32)
        for o in range(first, first + n_proj // 2):
            if not first:
                arrange(o + n_proj // 2)
            send = sends[o]
            at = (o - first) * rows
            send[:rows, :] = moved[at:at + rows]
            send[rows:rows + owned, :] = summed[o * owned:(o + 1) * owned]
            for b in range(rows // LANES):
                start = rows + owned + 2 * b
                send[start:start + 2, :] = told[:2, at + b * LANES:at + (b + 1) * LANES]


def hot_kernel(owned, year_ref, cohort_ref, product_ref, base_ref, *refs):
    planes, (hot_ref, level_ref), results, sem = refs[:3], refs[3:5], refs[5:8], refs[8]
    stores = [pltpu.make_async_copy(planes[i], results[i], sem.at[i]) for i in range(3)]
    for copy in stores:
        copy.start()
    _, label = relabel(cohort_ref[...], owned, lax.axis_index("proj"))
    label = label.astype(F32).T
    product = product_ref[...].astype(F32).T
    slot = iota((LANES, hot_ref.shape[1]), 1).astype(F32)
    rates = base_ref[pl.ds(year_ref[0], 1), :]
    for b in range(hot_ref.shape[0] // LANES):
        span = slice(b * LANES, (b + 1) * LANES)
        hot_ref[span, :] = onehot(jnp.broadcast_to(label[:, b:b + 1], slot.shape), slot)
        kind = jnp.broadcast_to(product[:, b:b + 1], (LANES, rates.shape[1]))
        rate = jnp.sum(jnp.where(kind == slot[:, :rates.shape[1]], rates, 0.0), axis=1, keepdims=True)
        level_ref[span, :] = jnp.broadcast_to(rate, (LANES, LANES))
    for copy in stores:
        copy.wait()


def paths_kernel(shocks_ref, paths_ref):
    sources, funds, horizon, width = shocks_ref.shape
    count = sources * width
    which = iota((2 * funds, width), 0)
    for b in range(sources):
        total = jnp.zeros((funds, width), F32)
        for h in range(horizon):
            total = total + shocks_ref[b, :, h, :]
            p1, p2, p3 = split(total, 3)
            ones = jnp.where(which < 3, float(h + 1), jnp.where(which < 6, 1.0, 0.0))
            full = jnp.concatenate([p1, p1, p2, p2, p3, p1, ones], axis=0)
            start = h * count + b * width
            paths_ref[start:start + width, :] = full.T.astype(BF16)


def value_kernel(dims, vol_ref, sigma_ref, mix_ref, paths_ref, *rest):
    n_proj, owned, rows, horizon, group, step = dims
    received = rest[:n_proj]
    cost_ref, weighted, mixes, loads, spare, money = rest[n_proj:]
    funds, products = mix_ref.shape
    trials = paths_ref.shape[0] // horizon
    per = rows // LANES
    mix = mix_ref[...]
    mix = mix / jnp.sum(mix, axis=0, keepdims=True)
    tops, lows = [], []
    labels = []
    for o in range(n_proj):
        weighted[o * rows:(o + 1) * rows, :] = halves(received[o][:rows, :])
        for b in range(per):
            start = rows + owned + 2 * b
            facts = received[o][start:start + 2, :]
            hot = (jnp.broadcast_to(facts[0:1], (products, LANES)).astype(I32) == iota((products, LANES), 0)).astype(F32)
            share = lax.dot_general(mix, hot, (((1,), (0,)), ((), ())), precision=HIGHEST, preferred_element_type=F32)
            top, low = split(share, 2)
            tops.append(top)
            lows.append(low)
            labels.append(facts[1:2].astype(I32))
    spans = n_proj * per
    for b in range(spans):
        mixes[0, b] = tops[b]
        mixes[1, b] = lows[b]
    same = (iota((funds, funds), 0) == iota((funds, funds), 1)).astype(F32)
    vol = jnp.broadcast_to(jnp.sum(same * vol_ref[...], axis=1, keepdims=True), (funds, LANES))
    sigma = sigma_ref[...]
    scale = sigma * LOG2E
    slope = -0.5 * sigma * sigma * LOG2E
    which = iota((funds, LANES), 0)

    def prepare(i, loads):
        first = i * group
        sides = []
        for part in range(2):
            wide = []
            for b in range(spans):
                share = mixes[part, b]
                wide.append(jnp.concatenate(
                    [jnp.where(labels[b] == first + c, share, 0.0) for c in range(group)], axis=0).astype(BF16))
            sides.append(jnp.concatenate(wide, axis=1))
        sums = join(dot(sides[0], weighted[...]) + dot(sides[1], weighted[...]))
        span = pl.ds(pl.multiple_of(rows + first, 8), group)
        secured = received[0][span, :]
        for o in range(1, n_proj):
            secured = secured + received[o][span, :]
        for c in range(group):
            part = sums[c * funds:(c + 1) * funds]
            inverse = 1.0 / jnp.sum(part, axis=0, keepdims=True)
            load = part * inverse * vol
            ratio = secured[c:c + 1] * inverse
            money[pl.ds(first + c, 1), :] = ratio
            spread = jnp.sum(load * load, axis=0, keepdims=True)
            w1, w2, w3 = split(load * scale, 3)
            d = split(slope * spread, 3) + split(-LOG2E * jnp.log(ratio), 3)
            extra = jnp.zeros((funds, LANES), F32)
            for k in range(6):
                extra = jnp.where(which == k, d[k], extra)
            full = jnp.concatenate([w1, w2, w1, w2, w1, w3, extra, jnp.zeros_like(extra)], axis=0)
            loads[:, c * LANES:(c + 1) * LANES] = full.astype(BF16)

    def value(i, loads):
        right = loads[...]
        total = None
        for h in range(horizon):
            reach = jnp.zeros((8, group * LANES), F32)
            for s in range(trials // step):
                left = paths_ref[h * trials + s * step:h * trials + (s + 1) * step, :]
                kept = jnp.exp2(jnp.minimum(dot(left, right), 0.0))
                reach = reach + jnp.sum(kept.reshape(step // 8, 8, group * LANES), axis=0)
            part = (float(trials) - jnp.sum(reach, axis=0, keepdims=True)) * (DISCOUNT ** (h + 1) / trials)
            total = part if total is None else total + part
        for c in range(group):
            row = pl.ds(i * group + c, 1)
            cost_ref[row, :] = total[:, c * LANES:(c + 1) * LANES] * money[row, :]

    turns = owned // group
    prepare(0, loads)

    def pair(j, _):
        prepare(2 * j + 1, spare)
        value(2 * j, loads)
        prepare(jnp.minimum(2 * j + 2, turns - 1), loads)
        value(2 * j + 1, spare)
        return 0

    lax.fori_loop(0, turns // 2, pair, 0)


def rates(costs):
    return jnp.concatenate(
        [halves(LAPSE_FLOOR + LAPSE_SPAN * jax.nn.sigmoid(LAPSE_SLOPE * (LAPSE_PIVOT - cost[...]))) for cost in costs],
        axis=0)


def near_kernel(hot_ref, *rest):
    costs, out_ref = rest[:-1], rest[-1]
    factors = rates(costs)
    out_ref[...] = join(dot(hot_ref[:, :factors.shape[0]], factors))


def lapse_kernel(hot_ref, near_ref, level_ref, *rest):
    costs, (out_hbm, out, sem) = rest[:-3], rest[-3:]
    factors = rates(costs)
    first = hot_ref.shape[1] - factors.shape[0]
    chunk = 2 * LANES

    def flush(i):
        span = pl.ds(i * chunk, chunk)
        return pltpu.make_async_copy(out.at[span], out_hbm.at[span], sem.at[i])

    chunks = out.shape[0] // chunk
    for i in range(chunks):
        span = slice(i * chunk, (i + 1) * chunk)
        out[span, :] = level_ref[span, :] * (near_ref[span, :] + join(dot(hot_ref[span, first:], factors)))
        flush(i).start()
    for i in range(chunks):
        flush(i).wait()


def exchange(x, axis, offset):
    return lax.ppermute(x, axis, flips(lax.axis_size(axis), offset))


def flips(n, offset):
    return [(i, i ^ offset) for i in range(n)]


def body(fund_value, in_force, guarantee_base, lapse_rate, cohort, product, guarantee_type, returns, mix_table,
         fee_table, rollup_table, fund_vol, closing_sigma_figure, shocks, base_table, year_index):
    n_proj, n_scen = lax.axis_size("proj"), lax.axis_size("scen")
    points, width = fund_value.shape
    funds, _, _ = returns.shape
    horizon = shocks.shape[1]
    products, types = mix_table.shape[0], fee_table.shape[0]
    owned = COHORTS // n_proj
    rows = -(-points // n_proj // LANES) * LANES
    message = rows + owned + 8 * -(-2 * (rows // LANES) // 8)
    blocks = points // LANES
    plane = jax.ShapeDtypeStruct((points, width), F32)
    labels = cohort.reshape(blocks, LANES)
    mix = mix_table.T

    sheets = jnp.concatenate([shocks[None], exchange(shocks[None], "scen", 1)], axis=0)
    kinds = product.reshape(blocks, LANES)
    small = [labels, kinds, guarantee_type.reshape(blocks, LANES), fee_table.reshape(1, types),
             rollup_table.reshape(1, types), mix, returns.transpose(1, 0, 2)]
    big = [fund_value, in_force, guarantee_base, lapse_rate]
    outs = pl.pallas_call(
        functools.partial(project_kernel, (n_proj, owned, rows)),
        out_shape=[pltpu.VMEM((message, width), F32)] * n_proj + [pltpu.VMEM((points, width), F32)] * 3,
        in_specs=[HBM] * 11,
        out_specs=[VMEM] * (n_proj + 3),
        scratch_shapes=[pltpu.VMEM(x.shape, x.dtype) for x in small + big] + [
            pltpu.VMEM((3 * products * types, 3 * LANES), BF16),
            pltpu.VMEM((points, 3 * products * types), BF16),
            pltpu.VMEM((points, 2 * width), BF16),
            pltpu.VMEM((points, 2 * width), BF16),
            pltpu.VMEM((n_proj * rows, points), BF16),
            pltpu.VMEM((COHORTS, points), BF16),
            pltpu.VMEM((max(rows, owned), LANES), F32),
            pltpu.SemaphoreType.DMA((7,)),
            pltpu.SemaphoreType.DMA((4,)),
        ],
        compiler_params=limit(24), name="project",
    )(*[hbm(x) for x in small + big])
    sends, planes = outs[:n_proj], outs[n_proj:]

    sheets, *sends = lax.optimization_barrier((sheets, *sends))
    received = [sends[0]] + [vmem(exchange(sends[o], "proj", o)) for o in range(1, n_proj)]

    offset = 2
    while offset < n_scen:
        if 2 * offset >= n_scen:
            sheets, labels, year_index = lax.optimization_barrier((sheets, labels, year_index))
        sheets = jnp.concatenate([sheets, exchange(sheets, "scen", offset)], axis=0)
        offset *= 2
    trials = n_scen * shocks.shape[2]

    hot, level, fund_next, force_next, base_next = pl.pallas_call(
        functools.partial(hot_kernel, owned),
        out_shape=[pltpu.VMEM((points, COHORTS), BF16), pltpu.VMEM((points, width), F32)] + [plane] * 3,
        in_specs=[pl.BlockSpec(memory_space=pltpu.SMEM)] + [VMEM] * 6, out_specs=[VMEM] * 2 + [HBM] * 3,
        scratch_shapes=[pltpu.SemaphoreType.DMA((3,))],
        compiler_params=limit(8), name="cohort_hot",
    )(year_index, labels, kinds, base_table, *planes)
    left = pl.pallas_call(
        paths_kernel,
        out_shape=pltpu.VMEM((horizon * trials, DEPTH), BF16),
        in_specs=[VMEM], out_specs=VMEM, compiler_params=limit(8), name="paths",
    )(vmem(sheets))
    left, hot = lax.optimization_barrier((left, hot))

    group = 16
    cost = pl.pallas_call(
        functools.partial(value_kernel, (n_proj, owned, rows, horizon, group, 64)),
        out_shape=pltpu.VMEM((owned, width), F32),
        in_specs=[VMEM] * (4 + n_proj), out_specs=VMEM,
        scratch_shapes=[
            pltpu.VMEM((n_proj * rows, 2 * width), BF16),
            pltpu.VMEM((2, n_proj * rows // LANES, funds, LANES), F32),
            pltpu.VMEM((DEPTH, group * LANES), BF16),
            pltpu.VMEM((DEPTH, group * LANES), BF16),
            pltpu.VMEM((owned, width), F32),
        ],
        compiler_params=limit(24), name="value",
    )(hbm(fund_vol.reshape(1, funds)), hbm(closing_sigma_figure.reshape(1, width)), hbm(mix), left, *received)

    costs = [cost]
    for o in range(1, n_proj):
        near = o % 2 and o > 1
        costs.append(exchange(costs[o - 1] if near else cost, "proj", 1 if near else o))
    costs = [cost] + [vmem(x) for x in costs[1:]]
    near = pl.pallas_call(
        near_kernel,
        out_shape=pltpu.VMEM((points, width), F32), in_specs=[VMEM] * 3, out_specs=VMEM,
        compiler_params=limit(8), name="near",
    )(hot, *costs[:2])
    lapse_next = pl.pallas_call(
        lapse_kernel,
        out_shape=plane, in_specs=[VMEM] * (1 + n_proj), out_specs=HBM,
        scratch_shapes=[pltpu.VMEM((points, width), F32), pltpu.SemaphoreType.DMA((points // (2 * LANES),))],
        compiler_params=limit(16), name="lapse",
    )(hot, near, level, *costs[2:])
    return fund_next, force_next, base_next, lapse_next, cost


def solution(mesh):
    both, proj = P("proj", "scen"), P("proj")
    paths = P(None, None, "scen")
    placed = (both,) * 4 + (proj,) * 3 + (paths, P(), P(), P(), P(), P("scen"), paths, P(), P())
    return jax.shard_map(body, mesh=mesh, in_specs=placed, out_specs=(both,) * 5, check_vma=False)
```

```python
import functools
import math

import jax
import jax.numpy as jnp
from jax import lax
from jax.experimental import pallas as pl
from jax.experimental.pallas import tpu as pltpu
from jax.sharding import PartitionSpec as P


COHORTS = 512
MONTHS_PER_YEAR = 12.0
DISCOUNT = 0.96
LAPSE_FLOOR, LAPSE_SPAN, LAPSE_SLOPE, LAPSE_PIVOT = 0.3, 2.0, 5.0, 0.4
LOG2E = 1.0 / math.log(2.0)
LANES = 128
DEPTH = 64
HIGHEST = lax.Precision.HIGHEST
F32, BF16, I32 = jnp.float32, jnp.bfloat16, jnp.int32
VMEM = pl.BlockSpec(memory_space=pltpu.VMEM)
HBM = pl.BlockSpec(memory_space=pltpu.HBM)


def dot(a, b):
    return jnp.dot(a, b, preferred_element_type=F32)


def iota(shape, axis):
    return lax.broadcasted_iota(I32, shape, axis)


def split(x, parts):
    out = []
    for _ in range(parts):
        top = x.astype(BF16).astype(F32)
        out.append(top)
        x = x - top
    return out


def halves(x):
    return jnp.concatenate(split(x, 2), axis=1).astype(BF16)


def join(x):
    return x[:, :LANES] + x[:, LANES:]


def onehot(row, ramp):
    return jnp.where(ramp == row, 1.0, 0.0).astype(BF16)


def vmem(x):
    return pltpu.with_memory_space_constraint(x, pltpu.VMEM)


def hbm(x):
    return pltpu.with_memory_space_constraint(x, pltpu.HBM)


def limit(mebibytes):
    return pltpu.CompilerParams(vmem_limit_bytes=mebibytes << 20)


def relabel(cohort, owned, me):
    shift = owned.bit_length() - 1
    owner = jnp.bitwise_xor(lax.shift_right_logical(cohort, shift), me)
    return owner, lax.shift_left(owner, shift) + jnp.bitwise_and(cohort, owned - 1)


def project_kernel(dims, *refs):
    n_proj, owned, rows = dims
    small, big = refs[:7], refs[7:11]
    sends, refs = refs[11:11 + n_proj], refs[11 + n_proj:]
    results, local_small, planes = refs[:3], refs[3:10], refs[10:14]
    table, hot, weighted, secured, move, gather, ramp, small_sem, in_sem = refs[14:]
    cohort_ref, product_ref, type_ref, fee_ref, roll_ref, mix_ref, returns_ref = local_small
    fund, force, guar, lapse = planes
    points = fund.shape[0]
    blocks = points // LANES
    months = returns_ref.shape[0]
    products, types = mix_ref.shape[1], fee_ref.shape[1]
    combos = products * types

    reads = [pltpu.make_async_copy(small[i], local_small[i], small_sem.at[i]) for i in range(7)]
    loads = [pltpu.make_async_copy(big[i], planes[i], in_sem.at[i]) for i in range(4)]
    for copy in reads + loads:
        copy.start()
    ramp[...] = iota(ramp.shape, 0).astype(F32)
    for copy in reads:
        copy.wait()

    cohort = cohort_ref[...]
    owner = relabel(cohort, owned, lax.axis_index("proj"))[0]
    local = jnp.bitwise_and(cohort, owned - 1).astype(F32)
    masks = jnp.concatenate([(owner == q).astype(F32) for q in range(n_proj)], axis=0)
    lower = (iota((LANES, LANES), 0) < iota((LANES, LANES), 1)).astype(BF16)
    before = dot(masks.astype(BF16), lower)
    count = dot(masks.astype(BF16), jnp.ones((LANES, LANES), BF16))
    size = n_proj * blocks
    r, c = iota((size, size), 0), iota((size, size), 1)
    shift = blocks.bit_length() - 1
    ahead = (lax.shift_right_logical(r, shift) == lax.shift_right_logical(c, shift)) & (c < r)
    before = before + dot(ahead.astype(BF16), count.astype(BF16))

    mix = mix_ref[...].T
    mix = mix / jnp.sum(mix, axis=1, keepdims=True)
    shares = [jnp.broadcast_to(mix[:, f:f + 1], (products, LANES)) for f in range(mix.shape[1])]
    wide = (products, LANES)
    keeps = [jnp.broadcast_to(1.0 - fee_ref[:, g:g + 1], wide) for g in range(types)]
    rolls = [jnp.broadcast_to(1.0 + roll_ref[:, g:g + 1] / MONTHS_PER_YEAR, wide) for g in range(types)]
    held = [jnp.ones(wide, F32)] * types
    best = [jnp.zeros(wide, F32)] * types
    rolled = [jnp.ones(wide, F32)] * types
    for t in range(months):
        month = returns_ref[t]
        growth = 1.0 + sum(share * month[f:f + 1] for f, share in enumerate(shares))
        for g in range(types):
            held[g] = held[g] * growth * keeps[g]
            best[g] = jnp.maximum(best[g] * rolls[g], held[g])
            rolled[g] = rolled[g] * rolls[g]
    for column, value in enumerate((held, best, rolled)):
        for i, part in enumerate(split(jnp.concatenate(value, axis=0), 3)):
            table[i * combos:(i + 1) * combos, column * LANES:(column + 1) * LANES] = part.astype(BF16)

    combo = (type_ref[...] * products + product_ref[...]).astype(F32).T
    slot = iota((LANES, 3 * combos), 1)
    slot = (slot - combos * ((slot >= combos).astype(I32) + (slot >= 2 * combos).astype(I32))).astype(F32)
    for b in range(blocks):
        column = jnp.broadcast_to(combo[:, b:b + 1], slot.shape)
        hot[b * LANES:(b + 1) * LANES, :] = onehot(column, slot)

    def arrange(o):
        mine = masks[o * blocks:(o + 1) * blocks] > 0.0
        rank = jnp.where(mine, before[o * blocks:(o + 1) * blocks], -1.0)
        for b in range(blocks):
            move[o * rows:(o + 1) * rows, b * LANES:(b + 1) * LANES] = onehot(rank[b:b + 1], ramp[:rows, :])

    for o in range(n_proj):
        label = jnp.where(masks[o * blocks:(o + 1) * blocks] > 0.0, local, -1.0)
        for b in range(blocks):
            span = slice(b * LANES, (b + 1) * LANES)
            gather[o * owned:(o + 1) * owned, span] = onehot(label[b:b + 1], ramp[:owned, :])
    for o in range(n_proj // 2):
        arrange(o)
    kind = product_ref[...].astype(F32)
    which = iota((16, LANES), 0)
    facts = jnp.concatenate(
        [jnp.where(which == 0, kind[b:b + 1], jnp.where(which == 1, local[b:b + 1], 0.0)) for b in range(blocks)],
        axis=1).astype(BF16)

    for copy in loads:
        copy.wait()
    factors = dot(hot[...], table[...])
    stay = 1.0 - lapse[...] / MONTHS_PER_YEAR
    stay = stay * stay * stay
    stay = stay * stay
    n = force[...] * (stay * stay)
    f = fund[...]
    g = jnp.maximum(guar[...] * factors[:, 2 * LANES:3 * LANES], f * factors[:, LANES:2 * LANES])
    f = f * factors[:, :LANES]
    for result, value in zip(results, (f, n, g)):
        result[...] = value
    weighted[...] = halves(n * f)
    secured[...] = halves(n * g)
    summed = join(dot(gather[...], secured[...]))
    for first in (0, n_proj // 2):
        span = slice(first * rows, (first + n_proj // 2) * rows)
        moved = join(dot(move[span, :], weighted[...]))
        told = lax.dot_general(facts, move[span, :], (((1,), (1,)), ((), ())), preferred_element_type=F32)
        for o in range(first, first + n_proj // 2):
            if not first:
                arrange(o + n_proj // 2)
            send = sends[o]
            at = (o - first) * rows
            send[:rows, :] = moved[at:at + rows]
            send[rows:rows + owned, :] = summed[o * owned:(o + 1) * owned]
            for b in range(rows // LANES):
                start = rows + owned + 2 * b
                send[start:start + 2, :] = told[:2, at + b * LANES:at + (b + 1) * LANES]


def hot_kernel(owned, cohort_ref, *refs):
    planes, hot_ref, results, sem = refs[:3], refs[3], refs[4:7], refs[7]
    stores = [pltpu.make_async_copy(planes[i], results[i], sem.at[i]) for i in range(3)]
    for copy in stores:
        copy.start()
    _, label = relabel(cohort_ref[...], owned, lax.axis_index("proj"))
    label = label.astype(F32).T
    slot = iota((LANES, hot_ref.shape[1]), 1).astype(F32)
    for b in range(hot_ref.shape[0] // LANES):
        hot_ref[b * LANES:(b + 1) * LANES, :] = onehot(jnp.broadcast_to(label[:, b:b + 1], slot.shape), slot)
    for copy in stores:
        copy.wait()


def level_kernel(year_ref, product_ref, base_ref, level_ref):
    product = product_ref[...].astype(F32).T
    rates = base_ref[pl.ds(year_ref[0], 1), :]
    shape = (LANES, rates.shape[1])
    slot = iota(shape, 1).astype(F32)
    for b in range(level_ref.shape[0] // LANES):
        kind = jnp.broadcast_to(product[:, b:b + 1], shape)
        rate = jnp.sum(jnp.where(kind == slot, rates, 0.0), axis=1, keepdims=True)
        level_ref[b * LANES:(b + 1) * LANES, :] = jnp.broadcast_to(rate, (LANES, LANES))


def paths_kernel(shocks_ref, paths_ref):
    sources, funds, horizon, width = shocks_ref.shape
    count = sources * width
    which = iota((2 * funds, width), 0)
    for b in range(sources):
        total = jnp.zeros((funds, width), F32)
        for h in range(horizon):
            total = total + shocks_ref[b, :, h, :]
            p1, p2, p3 = split(total, 3)
            ones = jnp.where(which < 3, float(h + 1), jnp.where(which < 6, 1.0, 0.0))
            full = jnp.concatenate([p1, p1, p2, p2, p3, p1, ones], axis=0)
            start = h * count + b * width
            paths_ref[start:start + width, :] = full.T.astype(BF16)


def value_kernel(dims, vol_ref, sigma_ref, mix_ref, early_ref, late_ref, *rest):
    n_proj, owned, rows, horizon, group, step = dims
    received = rest[:n_proj]
    cost_ref, weighted, mixes, loads, spare, money = rest[n_proj:]
    funds, products = mix_ref.shape
    half = early_ref.shape[0] // horizon
    trials = 2 * half
    per = rows // LANES
    mix = mix_ref[...]
    mix = mix / jnp.sum(mix, axis=0, keepdims=True)
    tops, lows = [], []
    labels = []
    for o in range(n_proj):
        weighted[o * rows:(o + 1) * rows, :] = halves(received[o][:rows, :])
        for b in range(per):
            start = rows + owned + 2 * b
            facts = received[o][start:start + 2, :]
            hot = (jnp.broadcast_to(facts[0:1], (products, LANES)).astype(I32) == iota((products, LANES), 0)).astype(F32)
            share = lax.dot_general(mix, hot, (((1,), (0,)), ((), ())), precision=HIGHEST, preferred_element_type=F32)
            top, low = split(share, 2)
            tops.append(top)
            lows.append(low)
            labels.append(facts[1:2].astype(I32))
    spans = n_proj * per
    for b in range(spans):
        mixes[0, b] = tops[b]
        mixes[1, b] = lows[b]
    same = (iota((funds, funds), 0) == iota((funds, funds), 1)).astype(F32)
    vol = jnp.broadcast_to(jnp.sum(same * vol_ref[...], axis=1, keepdims=True), (funds, LANES))
    sigma = sigma_ref[...]
    scale = sigma * LOG2E
    slope = -0.5 * sigma * sigma * LOG2E
    which = iota((funds, LANES), 0)

    def prepare(i, loads):
        first = i * group
        sides = []
        for part in range(2):
            wide = []
            for b in range(spans):
                share = mixes[part, b]
                wide.append(jnp.concatenate(
                    [jnp.where(labels[b] == first + c, share, 0.0) for c in range(group)], axis=0).astype(BF16))
            sides.append(jnp.concatenate(wide, axis=1))
        sums = join(dot(sides[0], weighted[...]) + dot(sides[1], weighted[...]))
        span = pl.ds(pl.multiple_of(rows + first, 8), group)
        secured = received[0][span, :]
        for o in range(1, n_proj):
            secured = secured + received[o][span, :]
        for c in range(group):
            part = sums[c * funds:(c + 1) * funds]
            inverse = 1.0 / jnp.sum(part, axis=0, keepdims=True)
            load = part * inverse * vol
            ratio = secured[c:c + 1] * inverse
            money[pl.ds(first + c, 1), :] = ratio
            spread = jnp.sum(load * load, axis=0, keepdims=True)
            w1, w2, w3 = split(load * scale, 3)
            d = split(slope * spread, 3) + split(-LOG2E * jnp.log(ratio), 3)
            extra = jnp.zeros((funds, LANES), F32)
            for k in range(6):
                extra = jnp.where(which == k, d[k], extra)
            full = jnp.concatenate([w1, w2, w1, w2, w1, w3, extra, jnp.zeros_like(extra)], axis=0)
            loads[:, c * LANES:(c + 1) * LANES] = full.astype(BF16)

    def value(i, loads):
        right = loads[...]
        total = None
        for h in range(horizon):
            reach = jnp.zeros((8, group * LANES), F32)
            for paths_ref in (early_ref, late_ref):
                for s in range(half // step):
                    left = paths_ref[h * half + s * step:h * half + (s + 1) * step, :]
                    kept = jnp.exp2(jnp.minimum(dot(left, right), 0.0))
                    reach = reach + jnp.sum(kept.reshape(step // 8, 8, group * LANES), axis=0)
            part = (float(trials) - jnp.sum(reach, axis=0, keepdims=True)) * (DISCOUNT ** (h + 1) / trials)
            total = part if total is None else total + part
        for c in range(group):
            row = pl.ds(i * group + c, 1)
            cost_ref[row, :] = total[:, c * LANES:(c + 1) * LANES] * money[row, :]

    turns = owned // group
    prepare(0, loads)

    def pair(j, _):
        prepare(2 * j + 1, spare)
        value(2 * j, loads)
        prepare(jnp.minimum(2 * j + 2, turns - 1), loads)
        value(2 * j + 1, spare)
        return 0

    lax.fori_loop(0, turns // 2, pair, 0)


def rates(costs):
    return jnp.concatenate(
        [halves(LAPSE_FLOOR + LAPSE_SPAN * jax.nn.sigmoid(LAPSE_SLOPE * (LAPSE_PIVOT - cost[...]))) for cost in costs],
        axis=0)


def near_kernel(hot_ref, *rest):
    costs, out_ref = rest[:-1], rest[-1]
    factors = rates(costs)
    out_ref[...] = join(dot(hot_ref[:, :factors.shape[0]], factors))


def lapse_kernel(hot_ref, near_ref, level_ref, *rest):
    costs, (out_hbm, out, sem) = rest[:-3], rest[-3:]
    factors = rates(costs)
    first = hot_ref.shape[1] - factors.shape[0]
    chunk = 2 * LANES

    def flush(i):
        span = pl.ds(i * chunk, chunk)
        return pltpu.make_async_copy(out.at[span], out_hbm.at[span], sem.at[i])

    chunks = out.shape[0] // chunk
    for i in range(chunks):
        span = slice(i * chunk, (i + 1) * chunk)
        out[span, :] = level_ref[span, :] * (near_ref[span, :] + join(dot(hot_ref[span, first:], factors)))
        flush(i).start()
    for i in range(chunks):
        flush(i).wait()


def exchange(x, axis, offset):
    return lax.ppermute(x, axis, flips(lax.axis_size(axis), offset))


def flips(n, offset):
    return [(i, i ^ offset) for i in range(n)]


def body(fund_value, in_force, guarantee_base, lapse_rate, cohort, product, guarantee_type, returns, mix_table,
         fee_table, rollup_table, fund_vol, closing_sigma_figure, shocks, base_table, year_index):
    n_proj, n_scen = lax.axis_size("proj"), lax.axis_size("scen")
    points, width = fund_value.shape
    funds, _, _ = returns.shape
    horizon = shocks.shape[1]
    products, types = mix_table.shape[0], fee_table.shape[0]
    owned = COHORTS // n_proj
    rows = -(-points // n_proj // LANES) * LANES
    message = rows + owned + 8 * -(-2 * (rows // LANES) // 8)
    blocks = points // LANES
    plane = jax.ShapeDtypeStruct((points, width), F32)
    labels = cohort.reshape(blocks, LANES)
    mix = mix_table.T

    sheets = jnp.concatenate([shocks[None], exchange(shocks[None], "scen", 1)], axis=0)
    kinds = product.reshape(blocks, LANES)
    small = [labels, kinds, guarantee_type.reshape(blocks, LANES), fee_table.reshape(1, types),
             rollup_table.reshape(1, types), mix, returns.transpose(1, 0, 2)]
    big = [fund_value, in_force, guarantee_base, lapse_rate]
    outs = pl.pallas_call(
        functools.partial(project_kernel, (n_proj, owned, rows)),
        out_shape=[pltpu.VMEM((message, width), F32)] * n_proj + [pltpu.VMEM((points, width), F32)] * 3,
        in_specs=[HBM] * 11,
        out_specs=[VMEM] * (n_proj + 3),
        scratch_shapes=[pltpu.VMEM(x.shape, x.dtype) for x in small + big] + [
            pltpu.VMEM((3 * products * types, 3 * LANES), BF16),
            pltpu.VMEM((points, 3 * products * types), BF16),
            pltpu.VMEM((points, 2 * width), BF16),
            pltpu.VMEM((points, 2 * width), BF16),
            pltpu.VMEM((n_proj * rows, points), BF16),
            pltpu.VMEM((COHORTS, points), BF16),
            pltpu.VMEM((max(rows, owned), LANES), F32),
            pltpu.SemaphoreType.DMA((7,)),
            pltpu.SemaphoreType.DMA((4,)),
        ],
        compiler_params=limit(24), name="project",
    )(*[hbm(x) for x in small + big])
    sends, planes = outs[:n_proj], outs[n_proj:]

    sheets, *sends = lax.optimization_barrier((sheets, *sends))
    received = [sends[0]] + [vmem(exchange(sends[o], "proj", o)) for o in range(1, n_proj)]

    offset = 2
    while offset < n_scen:
        if 2 * offset >= n_scen:
            sheets, kinds, year_index = lax.optimization_barrier((sheets, kinds, year_index))
        late = exchange(sheets, "scen", offset)
        if 2 * offset < n_scen:
            sheets = jnp.concatenate([sheets, late], axis=0)
        offset *= 2
    trials = n_scen * shocks.shape[2]

    build = pl.pallas_call(
        functools.partial(hot_kernel, owned),
        out_shape=[pltpu.VMEM((points, COHORTS), BF16)] + [plane] * 3,
        in_specs=[VMEM] * 4, out_specs=[VMEM] + [HBM] * 3,
        scratch_shapes=[pltpu.SemaphoreType.DMA((3,))],
        compiler_params=limit(8), name="cohort_hot",
    )
    hot, fund_next, force_next, base_next = build(hbm(labels), *planes)
    level = pl.pallas_call(
        level_kernel,
        out_shape=pltpu.VMEM((points, width), F32),
        in_specs=[pl.BlockSpec(memory_space=pltpu.SMEM)] + [VMEM] * 2, out_specs=VMEM,
        compiler_params=limit(8), name="level",
    )(year_index, hbm(kinds), hbm(base_table))
    halved = [pl.pallas_call(
        paths_kernel,
        out_shape=pltpu.VMEM((horizon * trials // 2, DEPTH), BF16),
        in_specs=[VMEM], out_specs=VMEM, compiler_params=limit(8), name="paths",
    )(vmem(x)) for x in (sheets, late)]
    late, level = lax.optimization_barrier((halved[1], level))

    group = 16
    cost = pl.pallas_call(
        functools.partial(value_kernel, (n_proj, owned, rows, horizon, group, 64)),
        out_shape=pltpu.VMEM((owned, width), F32),
        in_specs=[VMEM] * (5 + n_proj), out_specs=VMEM,
        scratch_shapes=[
            pltpu.VMEM((n_proj * rows, 2 * width), BF16),
            pltpu.VMEM((2, n_proj * rows // LANES, funds, LANES), F32),
            pltpu.VMEM((DEPTH, group * LANES), BF16),
            pltpu.VMEM((DEPTH, group * LANES), BF16),
            pltpu.VMEM((owned, width), F32),
        ],
        compiler_params=limit(24), name="value",
    )(hbm(fund_vol.reshape(1, funds)), hbm(closing_sigma_figure.reshape(1, width)), hbm(mix), halved[0], late, *received)

    costs = [cost]
    for o in range(1, n_proj):
        near = o % 2 and o > 1
        costs.append(exchange(costs[o - 1] if near else cost, "proj", 1 if near else o))
    costs = [cost] + [vmem(x) for x in costs[1:]]
    near = pl.pallas_call(
        near_kernel,
        out_shape=pltpu.VMEM((points, width), F32), in_specs=[VMEM] * 3, out_specs=VMEM,
        compiler_params=limit(8), name="near",
    )(hot, *costs[:2])
    lapse_next = pl.pallas_call(
        lapse_kernel,
        out_shape=plane, in_specs=[VMEM] * (1 + n_proj), out_specs=HBM,
        scratch_shapes=[pltpu.VMEM((points, width), F32), pltpu.SemaphoreType.DMA((points // (2 * LANES),))],
        compiler_params=limit(16), name="lapse",
    )(hot, near, level, *costs[2:])
    return fund_next, force_next, base_next, lapse_next, cost


def solution(mesh):
    both, proj = P("proj", "scen"), P("proj")
    paths = P(None, None, "scen")
    placed = (both,) * 4 + (proj,) * 3 + (paths, P(), P(), P(), P(), P("scen"), paths, P(), P())
    return jax.shard_map(body, mesh=mesh, in_specs=placed, out_specs=(both,) * 5, check_vma=False)
```
